256 devices in a mesh: ctx: 16 (over y_hi, z), tp: 16 (over x, y_lo, core).
Axes of the slice: x: 4, y: 4 (y_hi: 2, y_lo: 2; y = y_hi * 2 + y_lo), z: 8, core: 2. Of those that a mesh axis runs over, the one named last changes fastest.
Arguments:
- hidden_in: bfloat16 [8192, 8192], P('ctx', 'tp'), may hold values from -30 to 30
- norm_gain: bfloat16 [8192], P('tp'), may hold values from 0.099609375 to 1.8984375
- w_query: bfloat16 [8192, 4096], P(None, 'tp'), may hold values from -1 to 1
- w_key: bfloat16 [8192, 1024], P(None, 'tp'), may hold values from -1 to 1
- w_value: bfloat16 [8192, 1024], P(None, 'tp'), may hold values from -0.0625 to 0.0625
- sign_bits: int32 [32, 128], P('tp'), may hold values from 0 to 1
- w_out: bfloat16 [4096, 8192], P(None, 'tp'), may hold values from -1 to 1
- teacher: bfloat16 [8192, 8192], P('ctx', 'tp'), may hold values from -30 to 30
Outputs:
- student: bfloat16 [8192, 8192], P('ctx', 'tp')
- row_loss: float32 [8192], P('ctx')
The draws below stay inside these ranges and needn't reach their ends.
Inputs may be any that keep to these rules, and one draw needn't show every extreme that they name: `sign_bits`: 1 stands for the sign +1 and 0 for -1.
All inputs are finite; a program needn't handle non-finite values.
Results may differ from the reference program's by a relative error of at most 0.012.
The reference program's roundings to bfloat16 on the way (of `quantized`, `queries`, `attended` and `rotated_q`) count: a program that leaves them out, or rounds other values in their place, can miss the bound.
Values may be sent and summed in bfloat16 or wider, within the bound.
A program may use at most 128 MiB of HBM per device.

```python
import math
import jax
import jax.numpy as jnp
from jax import lax

D = 8192
QH = 32
KVH = 8
HD = 128
GROUP = 128
TOK_DEV = 512
SEQ = 8192


def column_profile(lowest, highest):
    columns = jnp.arange(D, dtype=jnp.float32)
    return lowest * (highest / lowest) ** (columns / max(D - 1, 1))


def draw_hidden_in(key, part):
    row_scale = jnp.exp(jax.random.uniform(jax.random.fold_in(key, 2), (SEQ, 1), jnp.float32, math.log(0.5), math.log(5.0)))
    noise = jax.random.normal(jax.random.fold_in(key, 1), (SEQ, D), jnp.float32)
    rows = noise * column_profile(0.58, 1.73) * row_scale
    return jnp.clip(rows, -30.0, 30.0).astype(jnp.bfloat16)


def draw_w_query(key, part):
    entries = jax.random.normal(jax.random.fold_in(key, 11), (D, QH * HD), jnp.float32) * D ** (-0.5)
    return jnp.clip(entries, -1.0, 1.0).astype(jnp.bfloat16)


def draw_w_key(key, part):
    entries = jax.random.normal(jax.random.fold_in(key, 12), (D, KVH * HD), jnp.float32) * D ** (-0.5)
    return jnp.clip(entries, -1.0, 1.0).astype(jnp.bfloat16)


def draw_w_out(key, part):
    entries = jax.random.normal(jax.random.fold_in(key, 13), (QH * HD, D), jnp.float32) * (QH * HD) ** (-0.5)
    entries = entries * column_profile(0.3, 3.0)
    return jnp.clip(entries, -1.0, 1.0).astype(jnp.bfloat16)


def draw_teacher(key, part):
    entries = jax.random.normal(jax.random.fold_in(key, 14), (SEQ, D), jnp.float32) * column_profile(0.3, 3.0)
    return jnp.clip(entries, -30.0, 30.0).astype(jnp.bfloat16)


def plant(values, stream_key, least, high):
    longest = values.shape.index(max(values.shape))
    spots = []
    for shift in (0, 1):
        where = [jax.random.randint(jax.random.fold_in(stream_key, axis), (), 0, length) for axis, length in enumerate(values.shape)]
        where[longest] = (where[longest] + shift) % values.shape[longest]
        spots.append(tuple(where))
    return values.at[spots[0]].set(least).at[spots[1]].set(high)


def block_scale(key, extent, split, least, high):
    gain = 1.0
    for axis_at, blocks in split:
        heights = jax.random.uniform(jax.random.fold_in(jax.random.fold_in(key, 6), axis_at), (blocks,), jnp.float32, least / len(split), high / len(split))
        gain = gain * jnp.repeat(jnp.exp(heights), extent[axis_at] // blocks).reshape((-1,) + (1,) * (len(extent) - 1 - axis_at))
    return gain


def normal_values(rng, shape, scale, most, pieces=(), held_as=jnp.bfloat16):
    values = scale * jax.random.normal(rng, shape, jnp.float32)
    if pieces:
        values = values * block_scale(rng, shape, pieces, -0.22, 0.18)
    return jnp.clip(values, -most, most).astype(held_as)


def setup_inputs(seed: int = 0) -> dict:
    arg_keys = jax.random.split(jax.random.key(seed), 9)
    return {
        "hidden_in": draw_hidden_in(jax.random.fold_in(arg_keys[8], 71), 0),
        "norm_gain": jnp.clip(1.0 + 0.18 * jax.random.normal(arg_keys[1], (D,), jnp.float32), 0.099609375, 1.8984375).astype(jnp.bfloat16),
        "w_query": draw_w_query(jax.random.fold_in(arg_keys[8], 71), 0),
        "w_key": draw_w_key(jax.random.fold_in(arg_keys[8], 71), 0),
        "w_value": normal_values(arg_keys[4], (D, KVH * HD), D ** -0.5, 0.0625, ((1, 16),)),
        "sign_bits": plant(jax.random.randint(arg_keys[5], (QH, HD), 0, 2), jax.random.fold_in(arg_keys[5], 1), 0, 1).astype(jnp.int32),
        "w_out": draw_w_out(jax.random.fold_in(arg_keys[8], 71), 0),
        "teacher": draw_teacher(jax.random.fold_in(arg_keys[8], 71), 0),
    }


EPS_IN = 1e-05
EPS_OUT = 1e-06
CLIP_RATIO = 0.9

def clip_groups(values):
    lead_shape = values.shape[:-1]
    width = values.shape[-1]
    grouped = values.reshape(lead_shape + (width // GROUP, GROUP))
    limit = CLIP_RATIO * lax.optimization_barrier(jnp.max(jnp.abs(grouped), axis=-1, keepdims=True))
    return jnp.clip(grouped, -limit, limit).reshape(values.shape)

def hadamard(order, dtype):
    index_row = jnp.arange(order, dtype=jnp.int32)
    both_bits = index_row[:, None] & index_row[None, :]
    parity = jnp.zeros_like(both_bits)
    for bit_index in range(max(order - 1, 1).bit_length()):
        parity = parity ^ both_bits >> bit_index & 1
    return (1 - 2 * parity).astype(dtype)

def reference(hidden_in, norm_gain, w_query, w_key, w_value, sign_bits, w_out, teacher):
    inputs = hidden_in.astype(jnp.float32)
    mean_sq = lax.optimization_barrier(jnp.mean(inputs * inputs, axis=-1, keepdims=True))
    normed = inputs * lax.rsqrt(mean_sq + EPS_IN) * norm_gain.astype(jnp.float32)
    quantized = clip_groups(normed).astype(jnp.bfloat16)
    queries = jnp.dot(quantized, w_query, preferred_element_type=jnp.float32).astype(jnp.bfloat16)
    keys_all = jnp.dot(quantized, w_key, preferred_element_type=jnp.float32).astype(jnp.bfloat16)
    values_all = jnp.dot(quantized, w_value, preferred_element_type=jnp.float32).astype(jnp.bfloat16)
    group_size = QH // KVH
    block_count = SEQ // TOK_DEV
    positions = jnp.arange(SEQ, dtype=jnp.int32)
    score_scale = HD ** (-0.5)

    def one_head(head):
        kv_head = head // group_size
        head_queries = lax.dynamic_slice_in_dim(queries, head * HD, HD, 1)
        head_keys = lax.dynamic_slice_in_dim(keys_all, kv_head * HD, HD, 1)
        head_values = lax.dynamic_slice_in_dim(values_all, kv_head * HD, HD, 1)

        def one_block(block):
            block_queries = lax.dynamic_slice_in_dim(head_queries, block * TOK_DEV, TOK_DEV, 0)
            query_pos = block * TOK_DEV + jnp.arange(TOK_DEV, dtype=jnp.int32)
            scores = jnp.dot(block_queries, head_keys.T, preferred_element_type=jnp.float32) * score_scale
            causal = positions[None, :] <= query_pos[:, None]
            masked = jnp.where(causal, scores, -jnp.inf)
            highest = lax.optimization_barrier(jnp.max(masked, axis=-1, keepdims=True))
            weights = jnp.where(causal, jnp.exp(scores - highest), 0.0)
            total = lax.optimization_barrier(jnp.sum(weights, axis=-1, keepdims=True))
            mixed = jnp.dot(weights.astype(jnp.bfloat16), head_values, preferred_element_type=jnp.float32)
            return mixed / total
        return lax.map(one_block, jnp.arange(block_count, dtype=jnp.int32))
    per_head = lax.map(one_head, jnp.arange(QH, dtype=jnp.int32))
    attended = per_head.reshape(QH, SEQ, HD).transpose(1, 0, 2).astype(jnp.bfloat16)
    signs = (2 * sign_bits - 1).astype(jnp.float32)
    signed = attended.astype(jnp.float32) * signs[None, :, :]
    mixing = hadamard(QH, jnp.float32)
    rotated = jnp.einsum('hg,sgd->shd', mixing, signed, precision=lax.Precision.HIGHEST) * QH ** (-0.5)
    rotated_q = clip_groups(rotated.reshape(SEQ, QH * HD)).astype(jnp.bfloat16)
    branch = jnp.dot(rotated_q, w_out, preferred_element_type=jnp.float32)
    inverse = lax.rsqrt(lax.optimization_barrier(jnp.mean(branch * branch, axis=-1, keepdims=True)) + EPS_OUT)
    normal_rows = branch * inverse
    difference = normal_rows - teacher.astype(jnp.float32)
    row_loss = lax.optimization_barrier(jnp.mean(difference * difference, axis=-1))
    return (normal_rows.astype(jnp.bfloat16), row_loss)
```

```python
import functools

import jax
import jax.numpy as jnp
from jax import lax
from jax.experimental import pallas as pl
from jax.experimental.pallas import tpu as pltpu
from jax.sharding import PartitionSpec as P

MESH = pl.DeviceIdType.MESH
F32 = jnp.float32
BF16 = jnp.bfloat16

D = 8192
QH = 32
HD = 128
ROWS = 512
TP = 16
WIDTH = D // TP
EPS_IN = 1e-05
EPS_OUT = 1e-06
CLIP_RATIO = 0.9
FAR_BELOW = -1e30
LOG2E = 1.4426950408889634
VMEM_LIMIT = 62 * 1024 * 1024


def tp_id(x, y, core):
    return lax.rem(x + 8, 4) * 4 + y * 2 + core


def tp_coords():
    me = lax.axis_index("tp")
    return me // 4, lax.rem(me // 2, 2), lax.rem(me, 2)


class Gather:
    def __init__(self, own, buf, send, recv):
        self.own, self.buf, self.send, self.recv = own, buf, send, recv
        x, y, core = tp_coords()
        self.core = core
        self.me = tp_id(x, y, core)
        self.right, self.left = tp_id(x + 1, y, core), tp_id(x - 1, y, core)
        self.across, self.mate = tp_id(x, 1 - y, core), tp_id(x, y, 1 - core)
        self.slots = [
            tp_id(x - 1, y, core),
            tp_id(x + 1, y, core),
            tp_id(x, 1 - y, core),
            tp_id(x + 2, y, core),
            tp_id(x - 1, 1 - y, core),
            tp_id(x + 1, 1 - y, core),
            tp_id(x + 2, 1 - y, core),
        ]
        self.mate_slots = [self.mate] + [s + 1 - 2 * core for s in self.slots]

    def slot_of(self, kind):
        return self.slots[kind] if kind < 7 else self.mate_slots[kind - 7]

    def copy(self, piece, kind, slot, target, own=False):
        return pltpu.make_async_remote_copy(
            src_ref=self.own.at[piece] if own else self.buf.at[piece, slot],
            dst_ref=self.buf.at[piece, slot],
            send_sem=self.send.at[piece, kind],
            recv_sem=self.recv.at[piece, kind],
            device_id={"tp": target},
            device_id_type=MESH,
        )

    def start_own(self, piece):
        self.copy(piece, 0, self.me, self.right, True).start()
        self.copy(piece, 1, self.me, self.left, True).start()
        self.copy(piece, 2, self.me, self.across, True).start()
        self.copy(piece, 7, self.me, self.mate, True).start()

    def landed(self, piece, kind):
        self.copy(piece, kind, self.slot_of(kind), self.mate).wait_recv()

    def forward(self, piece, kind, as_kind, target):
        self.copy(piece, as_kind, self.slots[kind], target).start()

    def first(self, piece):
        odd = lax.rem(piece, 2)
        self.landed(piece, 0)

        @pl.when(odd == 0)
        def _():
            self.forward(piece, 0, 3, self.right)

        self.forward(piece, 0, 8, self.mate)
        self.landed(piece, 1)

        @pl.when(odd == 1)
        def _():
            self.forward(piece, 1, 3, self.left)

        self.forward(piece, 1, 9, self.mate)
        self.landed(piece, 2)
        self.forward(piece, 2, 4, self.right)
        self.forward(piece, 2, 5, self.left)
        self.forward(piece, 2, 10, self.mate)

    def second(self, piece):
        self.landed(piece, 3)
        self.forward(piece, 3, 6, self.across)
        self.forward(piece, 3, 11, self.mate)
        self.landed(piece, 4)
        self.forward(piece, 4, 12, self.mate)
        self.landed(piece, 5)
        self.forward(piece, 5, 13, self.mate)

    def third(self, piece):
        self.landed(piece, 6)
        self.forward(piece, 6, 14, self.mate)

    def mates_landed(self, piece, kinds):
        for kind in kinds:
            self.landed(piece, kind)

    def drain(self, pieces):
        def one(piece, carry):
            self.copy(piece, 0, self.me, self.right, True).wait_send()
            self.copy(piece, 1, self.me, self.left, True).wait_send()
            self.copy(piece, 2, self.me, self.across, True).wait_send()
            self.copy(piece, 7, self.me, self.mate, True).wait_send()
            for kind in (3, 4, 5, 6, 8, 9, 10, 11, 12, 13, 14):
                self.copy(piece, kind, self.me, self.mate).wait_send()
            return carry

        lax.fori_loop(0, pieces, one, 0)


def greet_tp():
    me = lax.axis_index("tp")
    barrier = pltpu.get_barrier_semaphore()

    def greet(j, carry):
        pl.semaphore_signal(barrier, inc=1, device_id={"tp": me ^ j}, device_id_type=MESH)
        return carry

    lax.fori_loop(1, TP, greet, 0)
    pl.semaphore_wait(barrier, TP - 1)


def push_copy(j, box, send, recv, incoming=False):
    me = lax.axis_index("tp")
    slot = me ^ j if incoming else me
    return pltpu.make_async_remote_copy(
        src_ref=box.at[slot],
        dst_ref=box.at[slot],
        send_sem=send.at[j],
        recv_sem=recv.at[j],
        device_id={"tp": me ^ j},
        device_id_type=MESH,
    )


def push_start(box, send, recv):
    def one(j, carry):
        push_copy(j, box, send, recv).start()
        return carry

    lax.fori_loop(1, TP, one, 0)


def push_wait(box, send, recv):
    def one(j, carry):
        push_copy(j, box, send, recv, True).wait_recv()
        return carry

    lax.fori_loop(1, TP, one, 0)

    def sent(j, carry):
        push_copy(j, box, send, recv).wait_send()
        return carry

    lax.fori_loop(1, TP, sent, 0)


def to_lanes(column):
    n = column.shape[0]
    return jnp.transpose(jnp.broadcast_to(column, (n, 128)))[0:1, :]


def to_rows(lanes):
    n = lanes.shape[1]
    return jnp.transpose(jnp.broadcast_to(lanes, (128, n)))


A_PIECES = 4
A_ROWS = ROWS // A_PIECES


def project_kernel(
    x_ref, gain_ref, wq_hbm, wk_hbm, wv_hbm, q_ref, kv_ref,
    buf, stats, wq, wk, wv, wkv, inv, accq, acckv,
    send, recv, ssend, srecv, wsend, wrecv, wsem,
):
    x, y, core = tp_coords()
    me = lax.axis_index("tp")
    load_q = pltpu.make_async_copy(wq_hbm, wq, wsem.at[0])
    load_k = pltpu.make_async_copy(wk_hbm, wk, wsem.at[1])
    load_v = pltpu.make_async_copy(wv_hbm, wv, wsem.at[2])
    load_k.start()
    load_v.start()
    load_q.start()

    for piece in range(A_PIECES):
        rows = x_ref[piece].astype(F32)
        total = jnp.sum(rows * rows, axis=1, keepdims=True)
        stats[me, 0:1, piece * A_ROWS : (piece + 1) * A_ROWS] = to_lanes(total)
    stats[me, 1:2, :] = gain_ref[...].astype(F32)

    greet_tp()
    gather = Gather(x_ref, buf, send, recv)
    push_start(stats, ssend, srecv)
    gather.start_own(0)
    gather.start_own(1)

    load_k.wait()
    load_v.wait()

    def join(i, carry):
        at = pl.ds(pl.multiple_of(i * WIDTH, WIDTH), WIDTH)
        wkv[core, at, :] = jnp.concatenate([wk[at, :], wv[at, :]], axis=1)
        return carry

    lax.fori_loop(0, D // WIDTH, join, 0)

    push_wait(stats, ssend, srecv)
    share = pltpu.make_async_remote_copy(
        src_ref=wkv.at[core],
        dst_ref=wkv.at[core],
        send_sem=wsend,
        recv_sem=wrecv,
        device_id={"tp": gather.mate},
        device_id_type=MESH,
    )
    share_in = pltpu.make_async_remote_copy(
        src_ref=wkv.at[1 - core],
        dst_ref=wkv.at[1 - core],
        send_sem=wsend,
        recv_sem=wrecv,
        device_id={"tp": gather.mate},
        device_id_type=MESH,
    )
    share.start()
    squares = stats[0, 0:1, :]
    for slot in range(1, TP):
        squares = squares + stats[slot, 0:1, :]
    scale = lax.rsqrt(squares / D + EPS_IN)
    for piece in range(A_PIECES):
        inv[piece] = to_rows(scale[:, piece * A_ROWS : (piece + 1) * A_ROWS])
    accq[...] = jnp.zeros_like(accq)
    acckv[...] = jnp.zeros_like(acckv)
    load_q.wait()
    share_in.wait_recv()

    def consume(piece, slot, own=False):
        at = pl.ds(pl.multiple_of(slot * WIDTH, WIDTH), WIDTH)
        gain = stats[slot, 1:2, :]
        parts = []
        for g in range(WIDTH // 128):
            lanes = slice(g * 128, (g + 1) * 128)
            values = (x_ref[piece, :, lanes] if own else buf[piece, slot, :, lanes]).astype(F32)
            values = values * inv[piece] * gain[:, lanes]
            limit = CLIP_RATIO * jnp.max(jnp.abs(values), axis=-1, keepdims=True)
            parts.append(jnp.clip(values, -limit, limit).astype(BF16))
        quantized = jnp.concatenate(parts, axis=1)
        accq[piece] += jnp.dot(quantized, wq[at, :], preferred_element_type=F32)

        @pl.when(lax.rem(piece, 2) == core)
        def _():
            both = jnp.concatenate([wkv[0, at, :], wkv[1, at, :]], axis=1)
            acckv[piece // 2] += jnp.dot(quantized, both, preferred_element_type=F32)

    def pick(options, i):
        value = options[0]
        for n, option in enumerate(options[1:]):
            value = jnp.where(i == n + 1, option, value)
        return value

    def consume_all(piece, slots):
        def one(i, carry):
            consume(piece, pick(slots, i))
            return carry

        lax.fori_loop(0, len(slots), one, 0)

    group1 = gather.slots[:3] + gather.mate_slots[:4]
    group2 = gather.slots[3:6] + gather.mate_slots[4:7]
    group3 = gather.slots[6:7] + gather.mate_slots[7:8]

    def step(t, carry):
        @pl.when(t < A_PIECES)
        def _():
            consume(t, me, True)
            gather.first(t)

        @pl.when(t + 2 < A_PIECES)
        def _():
            gather.start_own(t + 2)

        @pl.when((t >= 1) & (t <= A_PIECES))
        def _():
            gather.second(t - 1)

        @pl.when((t >= 2) & (t <= A_PIECES + 1))
        def _():
            gather.third(t - 2)

        @pl.when(t < A_PIECES)
        def _():
            gather.mates_landed(t, (7, 8, 9, 10))
            consume_all(t, group1)

        @pl.when((t >= 1) & (t <= A_PIECES))
        def _():
            gather.mates_landed(t - 1, (11, 12, 13))
            consume_all(t - 1, group2)

        @pl.when((t >= 2) & (t <= A_PIECES + 1))
        def _():
            gather.mates_landed(t - 2, (14,))
            consume_all(t - 2, group3)

        return carry

    lax.fori_loop(0, A_PIECES + 2, step, 0)
    for piece in range(A_PIECES):
        for head in range(2):
            q_ref[head, piece] = accq[piece, :, head * HD : (head + 1) * HD].astype(BF16)
    for part in range(2):
        done = acckv[part].astype(BF16)
        at = slice(part * A_ROWS, (part + 1) * A_ROWS)
        kv_ref[at, :] = jnp.concatenate(
            [done[:, 0:64], done[:, 128:192], done[:, 64:128], done[:, 192:256]], axis=1
        )
    share.wait_send()
    gather.drain(A_PIECES)


def project(x, gain, w_query, w_key, w_value):
    any_space = pl.BlockSpec(memory_space=pl.ANY)
    vmem = pl.BlockSpec(memory_space=pltpu.VMEM)
    dma = pltpu.SemaphoreType.DMA
    return pl.pallas_call(
        project_kernel,
        out_shape=(
            jax.ShapeDtypeStruct((2, A_PIECES, A_ROWS, HD), BF16),
            jax.ShapeDtypeStruct((2 * A_ROWS, 2 * HD), BF16),
        ),
        in_specs=[vmem, vmem, any_space, any_space, any_space],
        out_specs=(vmem, vmem),
        scratch_shapes=[
            pltpu.VMEM((A_PIECES, TP, A_ROWS, WIDTH), BF16),
            pltpu.VMEM((TP, 2, WIDTH), F32),
            pltpu.VMEM((D, 256), BF16),
            pltpu.VMEM((D, 64), BF16),
            pltpu.VMEM((D, 64), BF16),
            pltpu.VMEM((2, D, 128), BF16),
            pltpu.VMEM((A_PIECES, A_ROWS, 128), F32),
            pltpu.VMEM((A_PIECES, A_ROWS, 256), F32),
            pltpu.VMEM((2, A_ROWS, 256), F32),
            dma((A_PIECES, 15)),
            dma((A_PIECES, 15)),
            dma((TP,)),
            dma((TP,)),
            dma,
            dma,
            dma((3,)),
        ],
        compiler_params=pltpu.CompilerParams(
            collective_id=0, has_side_effects=True, vmem_limit_bytes=VMEM_LIMIT
        ),
        name="project",
    )(x.reshape(A_PIECES, A_ROWS, WIDTH), gain.reshape(1, WIDTH), w_query, w_key, w_value)


KEYS = 2 * A_ROWS
QROWS = 2 * ROWS
QCHUNK = 256


def attend_kernel(q_ref, kv_ref, sign_ref, out_ref, buf, top, total, acc, send, recv):
    ctx = lax.axis_index("ctx")
    core = lax.rem(lax.axis_index("tp"), 2)
    mate = lax.axis_index("tp") + 1 - 2 * core
    row, z = ctx // 8, lax.rem(ctx, 8)
    sense = 1 - 2 * core
    other = (1 - row) * 8 + z

    def along(r, delta):
        return r * 8 + lax.rem(z + delta + 16, 8)

    ahead, behind = along(row, sense), along(row, -sense)

    def copy(kind, block, half, target, own=False):
        return pltpu.make_async_remote_copy(
            src_ref=kv_ref if own else buf.at[block, half],
            dst_ref=buf.at[block, half],
            send_sem=send.at[kind],
            recv_sem=recv.at[kind],
            device_id=target,
            device_id_type=MESH,
        )

    to_mate, to_ahead, to_behind = {"tp": mate}, {"ctx": ahead}, {"ctx": behind}
    barrier = pltpu.get_barrier_semaphore()
    for target in (to_mate, to_ahead, to_behind, {"ctx": other}):
        pl.semaphore_signal(barrier, inc=1, device_id=target, device_id_type=MESH)
    pl.semaphore_wait(barrier, 4)

    copy(1, ctx, core, to_ahead, True).start()
    copy(9, ctx, core, to_behind, True).start()
    copy(0, ctx, core, {"ctx": other}, True).start()
    copy(15, ctx, core, to_mate, True).start()

    top[...] = jnp.full_like(top, FAR_BELOW)
    total[...] = jnp.zeros_like(total)
    acc[...] = jnp.zeros_like(acc)
    factor = HD ** (-0.5) * LOG2E

    def unit(keys, values, half, masked):
        for chunk in range(QROWS // QCHUNK):
            at = slice(chunk * QCHUNK, (chunk + 1) * QCHUNK)
            scores = lax.dot_general(
                q_ref[at, :], keys, (((1,), (1,)), ((), ())), preferred_element_type=F32
            )
            if masked:
                base = (chunk * QCHUNK) % ROWS
                q_pos = base + lax.broadcasted_iota(jnp.int32, (QCHUNK, KEYS), 0)
                k_row = lax.broadcasted_iota(jnp.int32, (QCHUNK, KEYS), 1)
                k_pos = (k_row // A_ROWS) * (2 * A_ROWS) + half * A_ROWS + lax.rem(k_row, A_ROWS)
                seen = k_pos <= q_pos
                scores = jnp.where(seen, scores, FAR_BELOW)
            high = jnp.max(scores, axis=-1, keepdims=True)
            before = top[at, :]
            now = jnp.maximum(before, jnp.broadcast_to(high, (QCHUNK, 128)))
            decay = jnp.exp2((before - now) * factor)
            shift = now * factor
            left = jnp.exp2(scores[:, :128] * factor - shift)
            right = jnp.exp2(scores[:, 128:] * factor - shift)
            if masked:
                left = jnp.where(seen[:, :128], left, 0.0)
                right = jnp.where(seen[:, 128:], right, 0.0)
            total[at, :] = decay * total[at, :] + (left + right)
            weights = jnp.concatenate([left.astype(BF16), right.astype(BF16)], axis=1)
            mixed = jnp.dot(weights, values, preferred_element_type=F32)
            acc[at, :] = decay * acc[at, :] + mixed
            top[at, :] = now

    unit(kv_ref[:, :HD], kv_ref[:, HD:], core, True)

    def landed(kind, block, half):
        copy(kind, block, half, to_mate).wait_recv()

    def earlier(block, half):
        @pl.when(block < ctx)
        def _():
            unit(buf[block, half, :, :HD], buf[block, half, :, HD:], half, False)

    landed(15, ctx, 1 - core)
    unit(buf[ctx, 1 - core, :, :HD], buf[ctx, 1 - core, :, HD:], 1 - core, True)

    def step(n, carry):
        d, r = n // 2 + 1, lax.rem(n, 2)
        its_row = jnp.where(r == 0, row, 1 - row)

        @pl.when(n == 1)
        def _():
            landed(0, other, core)
            copy(2, other, core, to_ahead).start()
            copy(10, other, core, to_behind).start()
            copy(16, other, core, to_mate).start()

        @pl.when(n < 8)
        def _():
            block = along(its_row, -sense * d)
            landed(1 + n, block, core)

            @pl.when(n < 6)
            def _():
                copy(3 + n, block, core, to_ahead).start()

            copy(17 + n, block, core, to_mate).start()

        @pl.when(n < 6)
        def _():
            block = along(its_row, sense * d)
            landed(9 + n, block, core)

            @pl.when(n < 4)
            def _():
                copy(11 + n, block, core, to_behind).start()

            copy(25 + n, block, core, to_mate).start()

        def one(u, carry):
            late = u // 2
            back = lax.rem(u, 2)
            m = n - late
            half = jnp.where(late == 1, 1 - core, core)
            its = jnp.where(lax.rem(m + 2, 2) == 0, row, 1 - row)
            dist = (m + 2) // 2
            flip = jnp.where(late == 1, -sense, sense)
            delta = jnp.where(back == 0, -flip, flip) * dist
            block = along(its, delta)
            valid = (m >= 0) & (m < jnp.where(back == 0, 8, 6))

            @pl.when(valid)
            def _():
                @pl.when(late == 1)
                def _():
                    landed(jnp.where(back == 0, 17, 25) + m, block, 1 - core)

                earlier(block, half)

            return carry

        lax.fori_loop(0, 4, one, 0)

        @pl.when(n == 1)
        def _():
            earlier(other, core)

        @pl.when(n == 2)
        def _():
            landed(16, other, 1 - core)
            earlier(other, 1 - core)

        return carry

    lax.fori_loop(0, 9, step, 0)

    for head in range(2):
        signs = (2 * sign_ref[head : head + 1, :] - 1).astype(F32)
        for chunk in range(ROWS // QCHUNK):
            at = slice(head * ROWS + chunk * QCHUNK, head * ROWS + (chunk + 1) * QCHUNK)
            whole = jnp.sum(total[at, :], axis=-1, keepdims=True)
            attended = (acc[at, :] / whole).astype(BF16)
            out_ref[chunk * QCHUNK : (chunk + 1) * QCHUNK, head * HD : (head + 1) * HD] = (
                attended.astype(F32) * signs
            ).astype(BF16)

    def drain(kind, carry):
        copy(kind, ctx, core, to_mate).wait_send()
        return carry

    lax.fori_loop(0, 31, drain, 0)


def attend(q, kv, sign_bits):
    vmem = pl.BlockSpec(memory_space=pltpu.VMEM)
    dma = pltpu.SemaphoreType.DMA
    return pl.pallas_call(
        attend_kernel,
        out_shape=jax.ShapeDtypeStruct((ROWS, 2 * HD), BF16),
        in_specs=[vmem, vmem, vmem],
        out_specs=vmem,
        scratch_shapes=[
            pltpu.VMEM((16, 2, KEYS, 2 * HD), BF16),
            pltpu.VMEM((QROWS, 128), F32),
            pltpu.VMEM((QROWS, 128), F32),
            pltpu.VMEM((QROWS, HD), F32),
            dma((31,)),
            dma((31,)),
        ],
        compiler_params=pltpu.CompilerParams(
            collective_id=1, has_side_effects=True, vmem_limit_bytes=VMEM_LIMIT
        ),
        name="attend",
    )(q.reshape(QROWS, HD), kv, sign_bits)


C_PIECES = 4
C_ROWS = ROWS // C_PIECES
C_WIDTH = 2 * HD
STRIP = 16


def output_kernel(
    s_ref, w_hbm, teacher_ref, out_ref, loss_ref,
    buf, w, rotated, branch, box1, box2,
    send, recv, send1, recv1, send2, recv2, wsem,
):
    me = lax.axis_index("tp")
    load = pltpu.make_async_copy(w_hbm, w, wsem)
    load.start()
    greet_tp()
    gather = Gather(s_ref, buf, send, recv)
    gather.start_own(0)
    gather.start_own(1)
    load.wait()

    def consume(piece):
        def strip(i, carry):
            at = pl.ds(pl.multiple_of(i * STRIP, STRIP), STRIP)
            heads = []
            for slot in range(TP):
                both = buf[piece, slot, at, :].astype(F32)
                heads += [both[:, :HD], both[:, HD:]]
            span = 1
            while span < QH:
                for h in range(QH):
                    if not h & span:
                        a, b = heads[h], heads[h + span]
                        heads[h], heads[h + span] = a + b, a - b
                span *= 2
            for h in range(QH):
                value = heads[h] * QH ** (-0.5)
                limit = CLIP_RATIO * jnp.max(jnp.abs(value), axis=-1, keepdims=True)
                rotated[at, h * HD : (h + 1) * HD] = jnp.clip(value, -limit, limit).astype(BF16)
            return carry

        lax.fori_loop(0, C_ROWS // STRIP, strip, 0)
        branch[piece] = jnp.dot(rotated[...], w[...], preferred_element_type=F32)

    def step(t, carry):
        @pl.when(t < C_PIECES)
        def _():
            here = pltpu.make_async_copy(s_ref.at[t], buf.at[t, me], wsem)
            here.start()
            gather.first(t)
            here.wait()

        @pl.when(t + 2 < C_PIECES)
        def _():
            gather.start_own(t + 2)

        @pl.when((t >= 1) & (t <= C_PIECES))
        def _():
            gather.second(t - 1)

        @pl.when((t >= 2) & (t <= C_PIECES + 1))
        def _():
            gather.third(t - 2)
            gather.mates_landed(t - 2, range(7, 15))
            consume(t - 2)

        return carry

    lax.fori_loop(0, C_PIECES + 2, step, 0)

    for piece in range(C_PIECES):
        rows = branch[piece]
        total = jnp.sum(rows * rows, axis=1, keepdims=True)
        box1[me, 0:1, piece * C_ROWS : (piece + 1) * C_ROWS] = to_lanes(total)
    push_start(box1, send1, recv1)
    gather.drain(C_PIECES)
    push_wait(box1, send1, recv1)
    squares = box1[0, 0:1, :]
    for slot in range(1, TP):
        squares = squares + box1[slot, 0:1, :]
    inverse = lax.rsqrt(squares / D + EPS_OUT)
    for piece in range(C_PIECES):
        scale = to_rows(inverse[:, piece * C_ROWS : (piece + 1) * C_ROWS])
        partial = jnp.zeros((C_ROWS, 128), F32)
        for g in range(WIDTH // 128):
            lanes = slice(g * 128, (g + 1) * 128)
            normal = branch[piece, :, lanes] * scale
            out_ref[piece, :, lanes] = normal.astype(BF16)
            difference = normal - teacher_ref[piece, :, lanes].astype(F32)
            partial = partial + difference * difference
        total = jnp.sum(partial, axis=1, keepdims=True)
        box2[me, 0:1, piece * C_ROWS : (piece + 1) * C_ROWS] = to_lanes(total)
    push_start(box2, send2, recv2)
    push_wait(box2, send2, recv2)
    loss = box2[0, 0:1, :]
    for slot in range(1, TP):
        loss = loss + box2[slot, 0:1, :]
    loss_ref[...] = loss / D


def output(signed, w_out, teacher):
    any_space = pl.BlockSpec(memory_space=pl.ANY)
    vmem = pl.BlockSpec(memory_space=pltpu.VMEM)
    dma = pltpu.SemaphoreType.DMA
    student, loss = pl.pallas_call(
        output_kernel,
        out_shape=(
            jax.ShapeDtypeStruct((C_PIECES, C_ROWS, WIDTH), BF16),
            jax.ShapeDtypeStruct((1, ROWS), F32),
        ),
        in_specs=[vmem, any_space, vmem],
        out_specs=(vmem, vmem),
        scratch_shapes=[
            pltpu.VMEM((C_PIECES, TP, C_ROWS, C_WIDTH), BF16),
            pltpu.VMEM((QH * HD, WIDTH), BF16),
            pltpu.VMEM((C_ROWS, QH * HD), BF16),
            pltpu.VMEM((C_PIECES, C_ROWS, WIDTH), F32),
            pltpu.VMEM((TP, 1, ROWS), F32),
            pltpu.VMEM((TP, 1, ROWS), F32),
            dma((C_PIECES, 15)),
            dma((C_PIECES, 15)),
            dma((TP,)),
            dma((TP,)),
            dma((TP,)),
            dma((TP,)),
            dma,
        ],
        compiler_params=pltpu.CompilerParams(
            collective_id=2, has_side_effects=True, vmem_limit_bytes=VMEM_LIMIT
        ),
        name="output",
    )(
        signed.reshape(C_PIECES, C_ROWS, C_WIDTH),
        w_out,
        teacher.reshape(C_PIECES, C_ROWS, WIDTH),
    )
    return student.reshape(ROWS, WIDTH), loss.reshape(ROWS)


def body(hidden_in, norm_gain, w_query, w_key, w_value, sign_bits, w_out, teacher):
    q, kv = project(hidden_in, norm_gain, w_query, w_key, w_value)
    signed = attend(q, kv, sign_bits)
    return output(signed, w_out, teacher)


def solution(mesh):
    in_specs = (
        P("ctx", "tp"),
        P("tp"),
        P(None, "tp"),
        P(None, "tp"),
        P(None, "tp"),
        P("tp", None),
        P(None, "tp"),
        P("ctx", "tp"),
    )
    out_specs = (P("ctx", "tp"), P("ctx"))
    return jax.shard_map(body, mesh=mesh, in_specs=in_specs, out_specs=out_specs, check_vma=False)
```

```python
import functools

import jax
import jax.numpy as jnp
from jax import lax
from jax.experimental import pallas as pl
from jax.experimental.pallas import tpu as pltpu
from jax.sharding import PartitionSpec as P

MESH = pl.DeviceIdType.MESH
F32 = jnp.float32
BF16 = jnp.bfloat16

D = 8192
QH = 32
HD = 128
ROWS = 512
TP = 16
WIDTH = D // TP
EPS_IN = 1e-05
EPS_OUT = 1e-06
CLIP_RATIO = 0.9
FAR_BELOW = -1e30
LOG2E = 1.4426950408889634
VMEM_LIMIT = 62 * 1024 * 1024


def tp_id(x, y, core):
    return lax.rem(x + 8, 4) * 4 + y * 2 + core


def tp_coords():
    me = lax.axis_index("tp")
    return me // 4, lax.rem(me // 2, 2), lax.rem(me, 2)


class Gather:
    def __init__(self, buf, send, recv):
        self.buf, self.send, self.recv = buf, send, recv
        x, y, core = tp_coords()
        self.core = core
        self.me = tp_id(x, y, core)
        self.right, self.left = tp_id(x + 1, y, core), tp_id(x - 1, y, core)
        self.across, self.mate = tp_id(x, 1 - y, core), tp_id(x, y, 1 - core)
        self.slots = [
            tp_id(x - 1, y, core),
            tp_id(x + 1, y, core),
            tp_id(x, 1 - y, core),
            tp_id(x + 2, y, core),
            tp_id(x - 1, 1 - y, core),
            tp_id(x + 1, 1 - y, core),
            tp_id(x + 2, 1 - y, core),
        ]
        self.mate_slots = [self.mate] + [s + 1 - 2 * core for s in self.slots]

    def slot_of(self, kind):
        return self.slots[kind] if kind < 7 else self.mate_slots[kind - 7]

    def copy(self, piece, kind, slot, target):
        return pltpu.make_async_remote_copy(
            src_ref=self.buf.at[piece, slot],
            dst_ref=self.buf.at[piece, slot],
            send_sem=self.send.at[piece, kind],
            recv_sem=self.recv.at[piece, kind],
            device_id={"tp": target},
            device_id_type=MESH,
        )

    def start_sideways(self, piece):
        self.copy(piece, 0, self.me, self.right).start()
        self.copy(piece, 1, self.me, self.left).start()

    def start_near(self, piece):
        self.copy(piece, 2, self.me, self.across).start()
        self.copy(piece, 7, self.me, self.mate).start()

    def landed(self, piece, kind):
        self.copy(piece, kind, self.slot_of(kind), self.mate).wait_recv()

    def forward(self, piece, kind, as_kind, target):
        self.copy(piece, as_kind, self.slots[kind], target).start()

    def from_sides(self, piece):
        self.landed(piece, 0)
        if piece % 2 == 0:
            self.forward(piece, 0, 3, self.right)
        self.forward(piece, 0, 8, self.mate)
        self.landed(piece, 1)
        if piece % 2 == 1:
            self.forward(piece, 1, 3, self.left)
        self.forward(piece, 1, 9, self.mate)

    def from_across(self, piece):
        self.landed(piece, 2)
        self.forward(piece, 2, 4, self.right)
        self.forward(piece, 2, 5, self.left)
        self.forward(piece, 2, 10, self.mate)

    def from_far(self, piece):
        self.landed(piece, 3)
        self.forward(piece, 3, 6, self.across)
        self.forward(piece, 3, 11, self.mate)

    def from_diagonal(self, piece):
        self.landed(piece, 4)
        self.forward(piece, 4, 12, self.mate)
        self.landed(piece, 5)
        self.forward(piece, 5, 13, self.mate)

    def from_far_across(self, piece):
        self.landed(piece, 6)
        self.forward(piece, 6, 14, self.mate)

    def mates_landed(self, piece, kinds):
        for kind in kinds:
            self.landed(piece, kind)

    def drain(self, pieces):
        def one(piece, carry):
            for kind in range(15):
                self.copy(piece, kind, self.me, self.mate).wait_send()
            return carry

        lax.fori_loop(0, pieces, one, 0)


def push_copy(j, box, send, recv, incoming=False):
    me = lax.axis_index("tp")
    slot = me ^ j if incoming else me
    return pltpu.make_async_remote_copy(
        src_ref=box.at[slot],
        dst_ref=box.at[slot],
        send_sem=send.at[j],
        recv_sem=recv.at[j],
        device_id={"tp": me ^ j},
        device_id_type=MESH,
    )


def push_start(box, send, recv):
    def one(j, carry):
        push_copy(j, box, send, recv).start()
        return carry

    lax.fori_loop(1, TP, one, 0)


def push_wait(box, send, recv):
    def one(j, carry):
        push_copy(j, box, send, recv, True).wait_recv()
        return carry

    lax.fori_loop(1, TP, one, 0)

    def sent(j, carry):
        push_copy(j, box, send, recv).wait_send()
        return carry

    lax.fori_loop(1, TP, sent, 0)


def to_lanes(column):
    n = column.shape[0]
    return jnp.transpose(jnp.broadcast_to(column, (n, 128)))[0:1, :]


def to_rows(lanes):
    n = lanes.shape[1]
    return jnp.transpose(jnp.broadcast_to(lanes, (128, n)))


PIECES = 4
PROWS = ROWS // PIECES
QROWS = 2 * ROWS
HALF = ROWS // 2
STRIP = 16


def pick(options, i):
    value = options[0]
    for n, option in enumerate(options[1:]):
        value = jnp.where(i == n + 1, option, value)
    return value


def block_kernel(
    x_hbm, gain_ref, wq_hbm, wk_hbm, wv_hbm, sign_ref, wo_hbm, teacher_hbm,
    student_hbm, loss_ref,
    xraw, xbuf, stats, wq, wkv, accq, acckv, q, kvbuf, top, total, acc,
    sbuf, wo, rotated, branch, teacher, student, box1, box2,
    xsend, xrecv, ksend, krecv, ssend, srecv,
    psend0, precv0, psend1, precv1, psend2, precv2, wsend, wrecv, load_sem, x_sem,
):
    me = lax.axis_index("tp")
    ctx = lax.axis_index("ctx")
    rows = Gather(xbuf, xsend, xrecv)
    core, mate = rows.core, rows.mate

    x_loads = [
        pltpu.make_async_copy(x_hbm.at[p], xraw.at[p], x_sem.at[p]) for p in range(PIECES)
    ]
    for load in x_loads:
        load.start()

    def half(base, whose):
        return pl.ds(pl.multiple_of(base + whose * 64, 64), 64)

    load_k = pltpu.make_async_copy(wk_hbm, wkv.at[half(0, core)], load_sem.at[0])
    load_v = pltpu.make_async_copy(wv_hbm, wkv.at[half(128, core)], load_sem.at[1])
    load_q = pltpu.make_async_copy(wq_hbm, wq, load_sem.at[2])
    load_o = pltpu.make_async_copy(wo_hbm, wo, load_sem.at[3])
    load_t = pltpu.make_async_copy(teacher_hbm, teacher, load_sem.at[4])
    load_k.start()
    load_v.start()
    load_q.start()

    row, z = ctx // 8, lax.rem(ctx, 8)
    sense = 1 - 2 * core
    other = (1 - row) * 8 + z

    def along(r, delta):
        return r * 8 + lax.rem(z + delta + 16, 8)

    to_ahead, to_behind = {"ctx": along(row, sense)}, {"ctx": along(row, -sense)}
    to_other, to_mate = {"ctx": other}, {"tp": mate}

    barrier = pltpu.get_barrier_semaphore()

    def greet(j, carry):
        pl.semaphore_signal(barrier, inc=1, device_id={"tp": me ^ j}, device_id_type=MESH)
        return carry

    lax.fori_loop(1, TP, greet, 0)
    for target in (to_ahead, to_behind, to_other):
        pl.semaphore_signal(barrier, inc=1, device_id=target, device_id_type=MESH)

    for p in range(PIECES):
        x_loads[p].wait()
        values = xraw[p].astype(F32)
        stats[me, 0:1, p * PROWS : (p + 1) * PROWS] = to_lanes(
            jnp.sum(values * values, axis=1, keepdims=True)
        )
    pl.semaphore_wait(barrier, TP - 1 + 3)

    push_start(stats, psend0, precv0)
    load_o.start()
    load_t.start()
    load_k.wait()
    load_v.wait()

    def share(base, whose, n):
        return pltpu.make_async_remote_copy(
            src_ref=wkv.at[half(base, whose)],
            dst_ref=wkv.at[half(base, whose)],
            send_sem=wsend.at[n],
            recv_sem=wrecv.at[n],
            device_id=to_mate,
            device_id_type=MESH,
        )

    share(0, core, 0).start()
    share(128, core, 1).start()
    push_wait(stats, psend0, precv0)
    squares = stats[0, 0:1, :]
    for slot in range(1, TP):
        squares = squares + stats[slot, 0:1, :]
    scale = lax.rsqrt(squares / D + EPS_IN)
    gain = gain_ref[...].astype(F32).reshape(1, WIDTH)
    for p in range(PIECES):
        by_row = to_rows(scale[:, p * PROWS : (p + 1) * PROWS])
        for g in range(WIDTH // 128):
            lanes = slice(g * 128, (g + 1) * 128)
            values = xraw[p, :, lanes].astype(F32) * by_row * gain[:, lanes]
            limit = CLIP_RATIO * jnp.max(jnp.abs(values), axis=-1, keepdims=True)
            xbuf[p, me, :, lanes] = jnp.clip(values, -limit, limit).astype(BF16)
    accq[...] = jnp.zeros_like(accq)
    acckv[...] = jnp.zeros_like(acckv)

    for p in range(PIECES):
        rows.start_sideways(p)
        rows.start_near(p)
    load_q.wait()
    share(0, 1 - core, 0).wait_recv()
    share(128, 1 - core, 1).wait_recv()

    def consume(part, chip):
        at = pl.ds(pl.multiple_of(chip * 2 * WIDTH, 2 * WIDTH), 2 * WIDTH)
        both = [
            jnp.concatenate([xbuf[2 * part, slot], xbuf[2 * part + 1, slot]], axis=0)
            for slot in (2 * chip, 2 * chip + 1)
        ]
        quantized = jnp.concatenate(both, axis=1)
        accq[part] += jnp.dot(quantized, wq[at, :], preferred_element_type=F32)

        @pl.when(core == part)
        def _():
            acckv[...] += lax.dot_general(
                quantized, wkv[:, at], (((1,), (1,)), ((), ())), preferred_element_type=F32
            )

    def consume_all(part, kinds):
        chips = []
        for kind in kinds:
            for p in (2 * part, 2 * part + 1):
                rows.landed(p, 7 if kind is None else 8 + kind)
            chips.append((me if kind is None else rows.slots[kind]) // 2)

        def one(i, carry):
            consume(part, pick(chips, i))
            return carry

        lax.fori_loop(0, len(chips), one, 0)

    def kcopy(kind, block, part, target):
        return pltpu.make_async_remote_copy(
            src_ref=kvbuf.at[block, part],
            dst_ref=kvbuf.at[block, part],
            send_sem=ksend.at[kind],
            recv_sem=krecv.at[kind],
            device_id=target,
            device_id_type=MESH,
        )

    def klanded(kind, block, part):
        kcopy(kind, block, part, to_mate).wait_recv()

    def start_ring():
        kcopy(1, ctx, core, to_ahead).start()
        kcopy(9, ctx, core, to_behind).start()
        kcopy(0, ctx, core, to_other).start()
        kcopy(15, ctx, core, to_mate).start()

    def hop(n):
        d = n // 2 + 1
        its_row = jnp.where(lax.rem(n, 2) == 0, row, 1 - row)

        @pl.when(n == 1)
        def _():
            klanded(0, other, core)
            kcopy(2, other, core, to_ahead).start()
            kcopy(10, other, core, to_behind).start()
            kcopy(16, other, core, to_mate).start()

        back = along(its_row, -sense * d)
        klanded(1 + n, back, core)

        @pl.when(n < 6)
        def _():
            kcopy(3 + n, back, core, to_ahead).start()

        kcopy(17 + n, back, core, to_mate).start()

        @pl.when(n < 6)
        def _():
            front = along(its_row, sense * d)
            klanded(9 + n, front, core)

            @pl.when(n < 4)
            def _():
                kcopy(11 + n, front, core, to_behind).start()

            kcopy(25 + n, front, core, to_mate).start()

    rows.from_sides(0)
    rows.from_sides(1)
    rows.from_across(0)
    consume_all(0, (None,))
    rows.from_sides(2)
    rows.from_sides(3)
    rows.from_across(1)
    rows.from_across(2)
    rows.from_across(3)
    consume_all(1, (None,))
    consume_all(0, (0, 1))
    rows.from_far(0)
    rows.from_far(1)
    consume_all(0, (2,))
    rows.from_diagonal(0)
    consume_all(1, (0, 1))
    rows.from_far(2)
    rows.from_far(3)
    rows.from_far_across(0)
    consume_all(1, (2,))
    consume_all(0, (3,))
    rows.from_far_across(1)
    rows.from_diagonal(1)
    consume_all(1, (3,))
    consume_all(0, (4, 5, 6))
    rows.from_far_across(2)
    rows.from_diagonal(2)
    rows.from_far_across(3)
    rows.from_diagonal(3)
    consume_all(1, (4, 5, 6))
    kvbuf[ctx, core] = acckv[...].astype(BF16)
    for part in range(2):
        for head in range(2):
            q[head * ROWS + part * HALF : head * ROWS + (part + 1) * HALF, :] = accq[
                part, :, head * HD : (head + 1) * HD
            ].astype(BF16)
    start_ring()

    top[...] = jnp.full_like(top, FAR_BELOW)
    total[...] = jnp.zeros_like(total)
    acc[...] = jnp.zeros_like(acc)
    factor = HD ** (-0.5) * LOG2E

    def attend(keys, values, head, masked):
        at = slice(head * ROWS, (head + 1) * ROWS)
        scores = lax.dot_general(
            q[at, :], keys, (((1,), (1,)), ((), ())), preferred_element_type=F32
        )
        if masked:
            seen = lax.broadcasted_iota(jnp.int32, (ROWS, ROWS), 1) <= lax.broadcasted_iota(
                jnp.int32, (ROWS, ROWS), 0
            )
            scores = jnp.where(seen, scores, FAR_BELOW)
        high = jnp.max(scores, axis=-1, keepdims=True)
        before = top[at, :]
        now = jnp.maximum(before, jnp.broadcast_to(high, (ROWS, 128)))
        decay = jnp.exp2((before - now) * factor)
        shift = now * factor
        weights = []
        for g in range(ROWS // 128):
            lanes = slice(g * 128, (g + 1) * 128)
            part = jnp.exp2(scores[:, lanes] * factor - shift)
            if masked:
                part = jnp.where(seen[:, lanes], part, 0.0)
            weights.append(part)
        total[at, :] = decay * total[at, :] + ((weights[0] + weights[1]) + (weights[2] + weights[3]))
        mixed = jnp.dot(
            jnp.concatenate([part.astype(BF16) for part in weights], axis=1),
            values,
            preferred_element_type=F32,
        )
        acc[at, :] = decay * acc[at, :] + mixed
        top[at, :] = now

    def attend_block(block, masked):
        both = kvbuf[block].reshape(ROWS, 2 * HD)
        for head in range(2):
            attend(both[:, :HD], both[:, HD:], head, masked)

    def units(n):
        d = n // 2 + 1
        its_row = jnp.where(lax.rem(n, 2) == 0, row, 1 - row)

        def one(side, carry):
            valid = (side == 0) | ((side == 1) & (n < 6)) | ((side == 2) & (n == 1))
            block = jnp.where(
                side == 2, other, along(its_row, jnp.where(side == 0, -sense, sense) * d)
            )
            kind = jnp.where(side == 2, 16, jnp.where((side == 0) & (n < 6), 25 + n, 17 + n))

            @pl.when(valid)
            def _():
                klanded(kind, block, 1 - core)

            @pl.when(valid & (block < ctx))
            def _():
                attend_block(block, False)

            return carry

        lax.fori_loop(0, 3, one, 0)

    klanded(15, ctx, 1 - core)
    attend_block(ctx, True)

    def ring_step(k, carry):
        @pl.when(k < 8)
        def _():
            hop(k)

        @pl.when(k > 0)
        def _():
            units(k - 1)

        return carry

    lax.fori_loop(0, 9, ring_step, 0)

    heads = Gather(sbuf, ssend, srecv)
    for p in range(PIECES):
        for head in range(2):
            signs = (2 * sign_ref[head : head + 1, :] - 1).astype(F32)
            at = slice(head * ROWS + p * PROWS, head * ROWS + (p + 1) * PROWS)
            whole = jnp.sum(total[at, :], axis=-1, keepdims=True)
            attended = (acc[at, :] / whole).astype(BF16)
            sbuf[p, me, :, head * HD : (head + 1) * HD] = (
                attended.astype(F32) * signs
            ).astype(BF16)

    for p in (0, 1):
        heads.start_sideways(p)
        heads.start_near(p)
    heads.start_near(2)
    heads.start_near(3)
    load_o.wait()
    load_t.wait()

    def rotate(p):
        heads.mates_landed(p, range(7, 15))

        def strip(i, carry):
            at = pl.ds(pl.multiple_of(i * STRIP, STRIP), STRIP)
            mix = []
            for slot in range(TP):
                both = sbuf[p, slot, at, :].astype(F32)
                mix += [both[:, :HD], both[:, HD:]]
            span = 1
            while span < QH:
                for h in range(QH):
                    if not h & span:
                        a, b = mix[h], mix[h + span]
                        mix[h], mix[h + span] = a + b, a - b
                span *= 2
            for h in range(QH):
                value = mix[h] * QH ** (-0.5)
                limit = CLIP_RATIO * jnp.max(jnp.abs(value), axis=-1, keepdims=True)
                rotated[p, at, h * HD : (h + 1) * HD] = jnp.clip(value, -limit, limit).astype(BF16)
            return carry

        lax.fori_loop(0, PROWS // STRIP, strip, 0)

    heads.from_sides(0)
    heads.from_across(0)
    heads.start_sideways(2)
    heads.start_sideways(3)
    heads.from_sides(1)
    heads.from_across(1)
    heads.from_far(0)
    heads.from_far(1)
    heads.from_diagonal(0)
    heads.from_sides(2)
    heads.from_across(2)
    heads.from_far_across(0)
    heads.from_sides(3)
    heads.from_across(3)
    rotate(0)
    heads.from_far_across(1)
    heads.from_diagonal(1)
    heads.from_far(2)
    heads.from_far(3)
    rotate(1)
    heads.from_diagonal(2)
    heads.from_far_across(2)
    heads.from_diagonal(3)
    heads.from_far_across(3)
    rotate(2)
    rotate(3)
    result = jnp.dot(
        rotated[...].reshape(ROWS, QH * HD), wo[...], preferred_element_type=F32
    )
    branch[...] = result.reshape(PIECES, PROWS, WIDTH)
    box1[me, 0:1, :] = to_lanes(jnp.sum(result * result, axis=1, keepdims=True))

    push_start(box1, psend1, precv1)
    rows.drain(PIECES)
    heads.drain(PIECES)
    share(0, core, 0).wait_send()
    share(128, core, 1).wait_send()

    def drain(kind, carry):
        kcopy(kind, ctx, core, to_mate).wait_send()
        return carry

    lax.fori_loop(0, 31, drain, 0)
    push_wait(box1, psend1, precv1)
    squares = box1[0, 0:1, :]
    for slot in range(1, TP):
        squares = squares + box1[slot, 0:1, :]
    inverse = lax.rsqrt(squares / D + EPS_OUT)
    for p in range(PIECES):
        by_row = to_rows(inverse[:, p * PROWS : (p + 1) * PROWS])
        partial = jnp.zeros((PROWS, 128), F32)
        for g in range(WIDTH // 128):
            lanes = slice(g * 128, (g + 1) * 128)
            normal = branch[p, :, lanes] * by_row
            student[p, :, lanes] = normal.astype(BF16)
            difference = normal - teacher[p, :, lanes].astype(F32)
            partial = partial + difference * difference
        box2[me, 0:1, p * PROWS : (p + 1) * PROWS] = to_lanes(
            jnp.sum(partial, axis=1, keepdims=True)
        )
    push_start(box2, psend2, precv2)
    store = pltpu.make_async_copy(student, student_hbm, x_sem.at[0])
    store.start()
    push_wait(box2, psend2, precv2)
    loss = box2[0, 0:1, :]
    for slot in range(1, TP):
        loss = loss + box2[slot, 0:1, :]
    loss_ref[...] = loss / D
    store.wait()


def block(x, gain, w_query, w_key, w_value, sign_bits, w_out, teacher):
    any_space = pl.BlockSpec(memory_space=pl.ANY)
    vmem = pl.BlockSpec(memory_space=pltpu.VMEM)
    dma = pltpu.SemaphoreType.DMA
    return pl.pallas_call(
        block_kernel,
        out_shape=(
            jax.ShapeDtypeStruct((PIECES, PROWS, WIDTH), BF16),
            jax.ShapeDtypeStruct((1, ROWS), F32),
        ),
        in_specs=[any_space, vmem, any_space, any_space, any_space, vmem, any_space, any_space],
        out_specs=(any_space, vmem),
        scratch_shapes=[
            pltpu.VMEM((PIECES, PROWS, WIDTH), BF16),
            pltpu.VMEM((PIECES, TP, PROWS, WIDTH), BF16),
            pltpu.VMEM((TP, 1, ROWS), F32),
            pltpu.VMEM((D, 256), BF16),
            pltpu.VMEM((256, D), BF16),
            pltpu.VMEM((2, HALF, 256), F32),
            pltpu.VMEM((HALF, 256), F32),
            pltpu.VMEM((QROWS, HD), BF16),
            pltpu.VMEM((16, 2, HALF, 2 * HD), BF16),
            pltpu.VMEM((QROWS, 128), F32),
            pltpu.VMEM((QROWS, 128), F32),
            pltpu.VMEM((QROWS, HD), F32),
            pltpu.VMEM((PIECES, TP, PROWS, 2 * HD), BF16),
            pltpu.VMEM((QH * HD, WIDTH), BF16),
            pltpu.VMEM((PIECES, PROWS, QH * HD), BF16),
            pltpu.VMEM((PIECES, PROWS, WIDTH), F32),
            pltpu.VMEM((PIECES, PROWS, WIDTH), BF16),
            pltpu.VMEM((PIECES, PROWS, WIDTH), BF16),
            pltpu.VMEM((TP, 1, ROWS), F32),
            pltpu.VMEM((TP, 1, ROWS), F32),
            dma((PIECES, 15)),
            dma((PIECES, 15)),
            dma((31,)),
            dma((31,)),
            dma((PIECES, 15)),
            dma((PIECES, 15)),
            dma((TP,)),
            dma((TP,)),
            dma((TP,)),
            dma((TP,)),
            dma((TP,)),
            dma((TP,)),
            dma((2,)),
            dma((2,)),
            dma((5,)),
            dma((PIECES,)),
        ],
        compiler_params=pltpu.CompilerParams(
            collective_id=0, has_side_effects=True, vmem_limit_bytes=VMEM_LIMIT
        ),
        name="block",
    )(
        x.reshape(PIECES, PROWS, WIDTH),
        gain,
        w_query,
        w_key.T,
        w_value.T,
        sign_bits,
        w_out,
        teacher.reshape(PIECES, PROWS, WIDTH),
    )


def hand_over_kernel(student_ref, loss_ref, student_out, loss_out):
    student_out[...] = student_ref[...]
    loss_out[...] = loss_ref[...].reshape(ROWS)


def hand_over(student, loss):
    vmem = pl.BlockSpec(memory_space=pltpu.VMEM)
    return pl.pallas_call(
        hand_over_kernel,
        out_shape=(
            jax.ShapeDtypeStruct((ROWS, WIDTH), BF16),
            jax.ShapeDtypeStruct((ROWS,), F32),
        ),
        in_specs=[vmem, vmem],
        out_specs=(vmem, vmem),
        name="hand_over",
    )(student.reshape(ROWS, WIDTH), loss)


def body(*arguments):
    return hand_over(*block(*arguments))


def solution(mesh):
    in_specs = (
        P("ctx", "tp"),
        P("tp"),
        P(None, "tp"),
        P(None, "tp"),
        P(None, "tp"),
        P("tp", None),
        P(None, "tp"),
        P("ctx", "tp"),
    )
    out_specs = (P("ctx", "tp"), P("ctx"))
    return jax.shard_map(body, mesh=mesh, in_specs=in_specs, out_specs=out_specs, check_vma=False)
```

```python
import functools

import jax
import jax.numpy as jnp
from jax import lax
from jax.experimental import pallas as pl
from jax.experimental.pallas import tpu as pltpu
from jax.sharding import PartitionSpec as P

MESH = pl.DeviceIdType.MESH
F32 = jnp.float32
BF16 = jnp.bfloat16

D = 8192
QH = 32
HD = 128
ROWS = 512
TP = 16
WIDTH = D // TP
EPS_IN = 1e-05
EPS_OUT = 1e-06
CLIP_RATIO = 0.9
FAR_BELOW = -1e30
LOG2E = 1.4426950408889634
VMEM_LIMIT = 62 * 1024 * 1024


def tp_id(x, y, core):
    return lax.rem(x + 8, 4) * 4 + y * 2 + core


def tp_coords():
    me = lax.axis_index("tp")
    return me // 4, lax.rem(me // 2, 2), lax.rem(me, 2)


class Gather:
    def __init__(self, buf, send, recv):
        self.buf, self.send, self.recv = buf, send, recv
        x, y, core = tp_coords()
        self.core = core
        self.me = tp_id(x, y, core)
        self.right, self.left = tp_id(x + 1, y, core), tp_id(x - 1, y, core)
        self.across, self.mate = tp_id(x, 1 - y, core), tp_id(x, y, 1 - core)
        self.slots = [
            tp_id(x - 1, y, core),
            tp_id(x + 1, y, core),
            tp_id(x, 1 - y, core),
            tp_id(x + 2, y, core),
            tp_id(x - 1, 1 - y, core),
            tp_id(x + 1, 1 - y, core),
            tp_id(x + 2, 1 - y, core),
        ]
        self.mate_slots = [self.mate] + [s + 1 - 2 * core for s in self.slots]

    def slot_of(self, kind):
        return self.slots[kind] if kind < 7 else self.mate_slots[kind - 7]

    def copy(self, piece, kind, slot, target):
        return pltpu.make_async_remote_copy(
            src_ref=self.buf.at[piece, slot],
            dst_ref=self.buf.at[piece, slot],
            send_sem=self.send.at[piece, kind],
            recv_sem=self.recv.at[piece, kind],
            device_id={"tp": target},
            device_id_type=MESH,
        )

    def start_sideways(self, piece):
        self.copy(piece, 0, self.me, self.right).start()
        self.copy(piece, 1, self.me, self.left).start()

    def start_near(self, piece):
        self.copy(piece, 2, self.me, self.across).start()
        self.copy(piece, 7, self.me, self.mate).start()

    def landed(self, piece, kind):
        self.copy(piece, kind, self.slot_of(kind), self.mate).wait_recv()

    def forward(self, piece, kind, as_kind, target):
        self.copy(piece, as_kind, self.slots[kind], target).start()

    def from_sides(self, piece):
        self.landed(piece, 0)
        if piece % 2 == 0:
            self.forward(piece, 0, 3, self.right)
        self.forward(piece, 0, 8, self.mate)
        self.landed(piece, 1)
        if piece % 2 == 1:
            self.forward(piece, 1, 3, self.left)
        self.forward(piece, 1, 9, self.mate)

    def from_across(self, piece):
        self.landed(piece, 2)
        self.forward(piece, 2, 4, self.right)
        self.forward(piece, 2, 5, self.left)
        self.forward(piece, 2, 10, self.mate)

    def from_far(self, piece):
        self.landed(piece, 3)
        self.forward(piece, 3, 6, self.across)
        self.forward(piece, 3, 11, self.mate)

    def from_diagonal(self, piece):
        self.landed(piece, 4)
        self.forward(piece, 4, 12, self.mate)
        self.landed(piece, 5)
        self.forward(piece, 5, 13, self.mate)

    def from_far_across(self, piece):
        self.landed(piece, 6)
        self.forward(piece, 6, 14, self.mate)

    def mates_landed(self, piece, kinds):
        for kind in kinds:
            self.landed(piece, kind)

    def drain(self, pieces):
        def one(piece, carry):
            for kind in range(15):
                self.copy(piece, kind, self.me, self.mate).wait_send()
            return carry

        lax.fori_loop(0, pieces, one, 0)


def push_copy(j, box, send, recv, incoming=False):
    me = lax.axis_index("tp")
    slot = me ^ j if incoming else me
    return pltpu.make_async_remote_copy(
        src_ref=box.at[slot],
        dst_ref=box.at[slot],
        send_sem=send.at[j],
        recv_sem=recv.at[j],
        device_id={"tp": me ^ j},
        device_id_type=MESH,
    )


def push_start(box, send, recv):
    def one(j, carry):
        push_copy(j, box, send, recv).start()
        return carry

    lax.fori_loop(1, TP, one, 0)


def push_wait(box, send, recv):
    def one(j, carry):
        push_copy(j, box, send, recv, True).wait_recv()
        return carry

    lax.fori_loop(1, TP, one, 0)

    def sent(j, carry):
        push_copy(j, box, send, recv).wait_send()
        return carry

    lax.fori_loop(1, TP, sent, 0)


def to_lanes(column):
    n = column.shape[0]
    return jnp.transpose(jnp.broadcast_to(column, (n, 128)))[0:1, :]


def to_rows(lanes):
    n = lanes.shape[1]
    return jnp.transpose(jnp.broadcast_to(lanes, (128, n)))


PIECES = 4
PROWS = ROWS // PIECES
QROWS = 2 * ROWS
HALF = ROWS // 2
STRIP = 16


def pick(options, i):
    value = options[0]
    for n, option in enumerate(options[1:]):
        value = jnp.where(i == n + 1, option, value)
    return value


def block_kernel(
    x_hbm, gain_ref, wq_hbm, wk_hbm, wv_hbm, sign_ref, wo_hbm, teacher_hbm,
    student_hbm, loss_ref,
    xbuf, stats, wq, wkv, inv, accq, acckv, q, kvbuf, top, total, acc,
    sbuf, wo, rotated, branch, teacher, student, box1, box2,
    xsend, xrecv, ksend, krecv, ssend, srecv,
    psend0, precv0, psend1, precv1, psend2, precv2, wsend, wrecv, load_sem, x_sem,
):
    me = lax.axis_index("tp")
    ctx = lax.axis_index("ctx")
    rows = Gather(xbuf, xsend, xrecv)
    core, mate = rows.core, rows.mate

    x_loads = [
        pltpu.make_async_copy(x_hbm.at[p], xbuf.at[p, me], x_sem.at[p]) for p in range(PIECES)
    ]
    for load in x_loads:
        load.start()

    def half(base, whose):
        return pl.ds(pl.multiple_of(base + whose * 64, 64), 64)

    load_k = pltpu.make_async_copy(wk_hbm, wkv.at[half(0, core)], load_sem.at[0])
    load_v = pltpu.make_async_copy(wv_hbm, wkv.at[half(128, core)], load_sem.at[1])
    load_q = pltpu.make_async_copy(wq_hbm, wq, load_sem.at[2])
    load_o = pltpu.make_async_copy(wo_hbm, wo, load_sem.at[3])
    load_t = pltpu.make_async_copy(teacher_hbm, teacher, load_sem.at[4])
    load_k.start()
    load_v.start()
    load_q.start()

    row, z = ctx // 8, lax.rem(ctx, 8)
    sense = 1 - 2 * core
    other = (1 - row) * 8 + z

    def along(r, delta):
        return r * 8 + lax.rem(z + delta + 16, 8)

    to_ahead, to_behind = {"ctx": along(row, sense)}, {"ctx": along(row, -sense)}
    to_other, to_mate = {"ctx": other}, {"tp": mate}

    barrier = pltpu.get_barrier_semaphore()

    def greet(j, carry):
        pl.semaphore_signal(barrier, inc=1, device_id={"tp": me ^ j}, device_id_type=MESH)
        return carry

    lax.fori_loop(1, TP, greet, 0)
    for target in (to_ahead, to_behind, to_other):
        pl.semaphore_signal(barrier, inc=1, device_id=target, device_id_type=MESH)

    for p in range(PIECES):
        x_loads[p].wait()
        values = xbuf[p, me].astype(F32)
        stats[me, 0:1, p * PROWS : (p + 1) * PROWS] = to_lanes(
            jnp.sum(values * values, axis=1, keepdims=True)
        )
    stats[me, 1:2, :] = gain_ref[...].astype(F32).reshape(1, WIDTH)
    pl.semaphore_wait(barrier, TP - 1 + 3)

    push_start(stats, psend0, precv0)
    for p in range(PIECES):
        rows.start_sideways(p)
        rows.start_near(p)
    load_o.start()
    load_t.start()
    load_k.wait()
    load_v.wait()

    def share(base, whose, n):
        return pltpu.make_async_remote_copy(
            src_ref=wkv.at[half(base, whose)],
            dst_ref=wkv.at[half(base, whose)],
            send_sem=wsend.at[n],
            recv_sem=wrecv.at[n],
            device_id=to_mate,
            device_id_type=MESH,
        )

    share(0, core, 0).start()
    share(128, core, 1).start()
    push_wait(stats, psend0, precv0)
    squares = stats[0, 0:1, :]
    for slot in range(1, TP):
        squares = squares + stats[slot, 0:1, :]
    scale = lax.rsqrt(squares / D + EPS_IN)
    for p in range(PIECES):
        inv[p] = to_rows(scale[:, p * PROWS : (p + 1) * PROWS])
    accq[...] = jnp.zeros_like(accq)
    acckv[...] = jnp.zeros_like(acckv)

    load_q.wait()
    share(0, 1 - core, 0).wait_recv()
    share(128, 1 - core, 1).wait_recv()

    def consume(part, chip):
        at = pl.ds(pl.multiple_of(chip * 2 * WIDTH, 2 * WIDTH), 2 * WIDTH)
        both = []
        for slot in (2 * chip, 2 * chip + 1):
            gain = stats[slot, 1:2, :]
            for g in range(WIDTH // 128):
                lanes = slice(g * 128, (g + 1) * 128)
                column = []
                for p in (2 * part, 2 * part + 1):
                    values = xbuf[p, slot, :, lanes].astype(F32) * inv[p] * gain[:, lanes]
                    limit = CLIP_RATIO * jnp.max(jnp.abs(values), axis=-1, keepdims=True)
                    column.append(jnp.clip(values, -limit, limit).astype(BF16))
                both.append(jnp.concatenate(column, axis=0))
        quantized = jnp.concatenate(both, axis=1)
        accq[part] += jnp.dot(quantized, wq[at, :], preferred_element_type=F32)

        @pl.when(core == part)
        def _():
            acckv[...] += lax.dot_general(
                quantized, wkv[:, at], (((1,), (1,)), ((), ())), preferred_element_type=F32
            )

    def consume_all(part, kinds):
        chips = []
        for kind in kinds:
            for p in (2 * part, 2 * part + 1):
                rows.landed(p, 7 if kind is None else 8 + kind)
            chips.append((me if kind is None else rows.slots[kind]) // 2)

        def one(i, carry):
            consume(part, pick(chips, i))
            return carry

        lax.fori_loop(0, len(chips), one, 0)

    def kcopy(kind, block, part, target, g):
        return pltpu.make_async_remote_copy(
            src_ref=kvbuf.at[block, part, g],
            dst_ref=kvbuf.at[block, part, g],
            send_sem=ksend.at[g, kind],
            recv_sem=krecv.at[g, kind],
            device_id=target,
            device_id_type=MESH,
        )

    def klanded(kind, block, part, g):
        kcopy(kind, block, part, to_mate, g).wait_recv()

    def start_ring():
        for g in range(2):
            kcopy(0, ctx, core, to_ahead, g).start()
            kcopy(4, ctx, core, to_behind, g).start()
            kcopy(7, ctx, core, to_other, g).start()
            kcopy(15, ctx, core, to_mate, g).start()

    rings = {
        0: (0, -1, ((1, to_ahead), (8, to_other))),
        4: (0, 1, ((5, to_behind), (9, to_other))),
        1: (0, -2, ((2, to_ahead), (10, to_other))),
        5: (0, 2, ((6, to_behind), (11, to_other))),
        2: (0, -3, ((3, to_ahead),)),
        6: (0, 3, ()),
        3: (0, -4, ()),
        7: (1, 0, ()),
        8: (1, -1, ()),
        9: (1, 1, ()),
        10: (1, -2, ((12, to_ahead),)),
        11: (1, 2, ((14, to_behind),)),
        12: (1, -3, ((13, to_ahead),)),
        14: (1, 3, ()),
        13: (1, -4, ()),
    }

    def pass_on(*kinds):
        for g in range(2):
            for kind in kinds:
                far_row, delta, targets = rings[kind]
                block = along(1 - row if far_row else row, sense * delta)
                klanded(kind, block, core, g)
                for as_kind, target in targets:
                    kcopy(as_kind, block, core, target, g).start()
                kcopy(16 + kind, block, core, to_mate, g).start()

    rows.from_sides(0)
    rows.from_sides(1)
    rows.from_across(0)
    consume_all(0, (None,))
    rows.from_sides(2)
    rows.from_sides(3)
    rows.from_across(1)
    rows.from_across(2)
    rows.from_across(3)
    consume_all(1, (None,))
    consume_all(0, (0, 1))
    rows.from_far(0)
    rows.from_far(1)
    consume_all(0, (2,))
    rows.from_diagonal(0)
    consume_all(1, (0, 1))
    rows.from_far(2)
    rows.from_far(3)
    rows.from_far_across(0)
    consume_all(1, (2,))
    consume_all(0, (3,))
    rows.from_far_across(1)
    rows.from_diagonal(1)
    consume_all(1, (3,))
    consume_all(0, (4, 5, 6))
    rows.from_far_across(2)
    rows.from_diagonal(2)
    rows.from_far_across(3)
    rows.from_diagonal(3)
    consume_all(1, (4, 5, 6))
    kvbuf[ctx, core] = acckv[...].astype(BF16).reshape(2, PROWS, 2 * HD)
    for part in range(2):
        for head in range(2):
            q[head * ROWS + part * HALF : head * ROWS + (part + 1) * HALF, :] = accq[
                part, :, head * HD : (head + 1) * HD
            ].astype(BF16)
    start_ring()

    top[...] = jnp.full_like(top, FAR_BELOW)
    total[...] = jnp.zeros_like(total)
    acc[...] = jnp.zeros_like(acc)
    factor = HD ** (-0.5) * LOG2E

    def attend(keys, values, head, masked):
        at = slice(head * ROWS, (head + 1) * ROWS)
        scores = lax.dot_general(
            q[at, :], keys, (((1,), (1,)), ((), ())), preferred_element_type=F32
        )
        if masked:
            seen = lax.broadcasted_iota(jnp.int32, (ROWS, ROWS), 1) <= lax.broadcasted_iota(
                jnp.int32, (ROWS, ROWS), 0
            )
            scores = jnp.where(seen, scores, FAR_BELOW)
        high = jnp.max(scores, axis=-1, keepdims=True)
        before = top[at, :]
        now = jnp.maximum(before, jnp.broadcast_to(high, (ROWS, 128)))
        decay = jnp.exp2((before - now) * factor)
        shift = now * factor
        weights = []
        for g in range(ROWS // 128):
            lanes = slice(g * 128, (g + 1) * 128)
            part = jnp.exp2(scores[:, lanes] * factor - shift)
            if masked:
                part = jnp.where(seen[:, lanes], part, 0.0)
            weights.append(part)
        total[at, :] = decay * total[at, :] + ((weights[0] + weights[1]) + (weights[2] + weights[3]))
        mixed = jnp.dot(
            jnp.concatenate([part.astype(BF16) for part in weights], axis=1),
            values,
            preferred_element_type=F32,
        )
        acc[at, :] = decay * acc[at, :] + mixed
        top[at, :] = now

    def attend_block(block, masked):
        both = kvbuf[block].reshape(ROWS, 2 * HD)
        for head in range(2):
            attend(both[:, :HD], both[:, HD:], head, masked)

    order = (0, 4, 7, 1, 5, 8, 9, 2, 6, 10, 11, 3, 12, 14, 13)
    twin = {0: 4, 1: 5, 2: 6, 3: 3, 4: 0, 5: 1, 6: 2, 7: 7, 8: 9, 9: 8, 10: 11, 11: 10, 12: 14, 13: 13, 14: 12}

    def unit(j, carry):
        far_row = pick([jnp.int32(rings[kind][0]) for kind in order], j)
        delta = pick([jnp.int32(rings[kind][1]) for kind in order], j)
        kind = pick([jnp.int32(16 + twin[kind]) for kind in order], j)
        block = along(jnp.where(far_row == 1, 1 - row, row), sense * delta)
        for g in range(2):
            klanded(kind, block, 1 - core, g)

        @pl.when(block < ctx)
        def _():
            attend_block(block, False)

        return carry

    for g in range(2):
        klanded(15, ctx, 1 - core, g)
    attend_block(ctx, True)

    steps = ((0, 4), (7, 1, 5), (8, 9, 2, 6), (10, 11, 3), (12, 14), (13,))

    def ring_step(k, carry):
        for i, kinds in enumerate(steps):
            pl.when(k == i)(functools.partial(pass_on, *kinds))
        low = jnp.maximum(3 * k - 4, 0)
        high = jnp.minimum(jnp.maximum(3 * k - 1, 0), 15)
        lax.fori_loop(low, high, unit, 0)
        return carry

    lax.fori_loop(0, len(steps) + 1, ring_step, 0)

    heads = Gather(sbuf, ssend, srecv)
    for p in range(PIECES):
        for head in range(2):
            signs = (2 * sign_ref[head : head + 1, :] - 1).astype(F32)
            at = slice(head * ROWS + p * PROWS, head * ROWS + (p + 1) * PROWS)
            whole = jnp.sum(total[at, :], axis=-1, keepdims=True)
            attended = (acc[at, :] / whole).astype(BF16)
            sbuf[p, me, :, head * HD : (head + 1) * HD] = (
                attended.astype(F32) * signs
            ).astype(BF16)

    for p in (0, 1):
        heads.start_sideways(p)
        heads.start_near(p)
    heads.start_near(2)
    heads.start_near(3)
    load_o.wait()
    load_t.wait()

    def rotate(p):
        heads.mates_landed(p, range(7, 15))

        def strip(i, carry):
            at = pl.ds(pl.multiple_of(i * STRIP, STRIP), STRIP)
            mix = []
            for slot in range(TP):
                both = sbuf[p, slot, at, :].astype(F32)
                mix += [both[:, :HD], both[:, HD:]]
            span = 1
            while span < QH:
                for h in range(QH):
                    if not h & span:
                        a, b = mix[h], mix[h + span]
                        mix[h], mix[h + span] = a + b, a - b
                span *= 2
            for h in range(QH):
                value = mix[h] * QH ** (-0.5)
                limit = CLIP_RATIO * jnp.max(jnp.abs(value), axis=-1, keepdims=True)
                rotated[p, at, h * HD : (h + 1) * HD] = jnp.clip(value, -limit, limit).astype(BF16)
            return carry

        lax.fori_loop(0, PROWS // STRIP, strip, 0)

    heads.from_sides(0)
    heads.from_across(0)
    heads.start_sideways(2)
    heads.start_sideways(3)
    heads.from_sides(1)
    heads.from_across(1)
    heads.from_far(0)
    heads.from_far(1)
    heads.from_diagonal(0)
    heads.from_sides(2)
    heads.from_across(2)
    heads.from_far_across(0)
    heads.from_sides(3)
    heads.from_across(3)
    rotate(0)
    heads.from_far_across(1)
    heads.from_diagonal(1)
    heads.from_far(2)
    heads.from_far(3)
    rotate(1)
    heads.from_diagonal(2)
    heads.from_far_across(2)
    rotate(2)
    heads.from_diagonal(3)
    heads.from_far_across(3)
    rotate(3)
    result = jnp.dot(
        rotated[...].reshape(ROWS, QH * HD), wo[...], preferred_element_type=F32
    )
    branch[...] = result.reshape(PIECES, PROWS, WIDTH)
    box1[me, 0:1, :] = to_lanes(jnp.sum(result * result, axis=1, keepdims=True))

    push_start(box1, psend1, precv1)
    rows.drain(PIECES)
    heads.drain(PIECES)
    share(0, core, 0).wait_send()
    share(128, core, 1).wait_send()

    def drain(kind, carry):
        for g in range(2):
            kcopy(kind, ctx, core, to_mate, g).wait_send()
        return carry

    lax.fori_loop(0, 31, drain, 0)
    push_wait(box1, psend1, precv1)
    squares = box1[0, 0:1, :]
    for slot in range(1, TP):
        squares = squares + box1[slot, 0:1, :]
    inverse = lax.rsqrt(squares / D + EPS_OUT)
    for p in range(PIECES):
        by_row = to_rows(inverse[:, p * PROWS : (p + 1) * PROWS])
        partial = jnp.zeros((PROWS, 128), F32)
        for g in range(WIDTH // 128):
            lanes = slice(g * 128, (g + 1) * 128)
            normal = branch[p, :, lanes] * by_row
            student[p, :, lanes] = normal.astype(BF16)
            difference = normal - teacher[p, :, lanes].astype(F32)
            partial = partial + difference * difference
        box2[me, 0:1, p * PROWS : (p + 1) * PROWS] = to_lanes(
            jnp.sum(partial, axis=1, keepdims=True)
        )
    push_start(box2, psend2, precv2)
    store = pltpu.make_async_copy(student, student_hbm, x_sem.at[0])
    store.start()
    push_wait(box2, psend2, precv2)
    loss = box2[0, 0:1, :]
    for slot in range(1, TP):
        loss = loss + box2[slot, 0:1, :]
    loss_ref[...] = loss / D
    store.wait()


def block(x, gain, w_query, w_key, w_value, sign_bits, w_out, teacher):
    any_space = pl.BlockSpec(memory_space=pl.ANY)
    vmem = pl.BlockSpec(memory_space=pltpu.VMEM)
    dma = pltpu.SemaphoreType.DMA
    return pl.pallas_call(
        block_kernel,
        out_shape=(
            jax.ShapeDtypeStruct((PIECES, PROWS, WIDTH), BF16),
            jax.ShapeDtypeStruct((1, ROWS), F32),
        ),
        in_specs=[any_space, vmem, any_space, any_space, any_space, vmem, any_space, any_space],
        out_specs=(any_space, vmem),
        scratch_shapes=[
            pltpu.VMEM((PIECES, TP, PROWS, WIDTH), BF16),
            pltpu.VMEM((TP, 2, ROWS), F32),
            pltpu.VMEM((D, 256), BF16),
            pltpu.VMEM((256, D), BF16),
            pltpu.VMEM((PIECES, PROWS, 128), F32),
            pltpu.VMEM((2, HALF, 256), F32),
            pltpu.VMEM((HALF, 256), F32),
            pltpu.VMEM((QROWS, HD), BF16),
            pltpu.VMEM((16, 2, 2, PROWS, 2 * HD), BF16),
            pltpu.VMEM((QROWS, 128), F32),
            pltpu.VMEM((QROWS, 128), F32),
            pltpu.VMEM((QROWS, HD), F32),
            pltpu.VMEM((PIECES, TP, PROWS, 2 * HD), BF16),
            pltpu.VMEM((QH * HD, WIDTH), BF16),
            pltpu.VMEM((PIECES, PROWS, QH * HD), BF16),
            pltpu.VMEM((PIECES, PROWS, WIDTH), F32),
            pltpu.VMEM((PIECES, PROWS, WIDTH), BF16),
            pltpu.VMEM((PIECES, PROWS, WIDTH), BF16),
            pltpu.VMEM((TP, 1, ROWS), F32),
            pltpu.VMEM((TP, 1, ROWS), F32),
            dma((PIECES, 15)),
            dma((PIECES, 15)),
            dma((2, 31)),
            dma((2, 31)),
            dma((PIECES, 15)),
            dma((PIECES, 15)),
            dma((TP,)),
            dma((TP,)),
            dma((TP,)),
            dma((TP,)),
            dma((TP,)),
            dma((TP,)),
            dma((2,)),
            dma((2,)),
            dma((5,)),
            dma((PIECES,)),
        ],
        compiler_params=pltpu.CompilerParams(
            collective_id=0, has_side_effects=True, vmem_limit_bytes=VMEM_LIMIT
        ),
        name="block",
    )(
        x.reshape(PIECES, PROWS, WIDTH),
        gain,
        w_query,
        w_key.T,
        w_value.T,
        sign_bits,
        w_out,
        teacher.reshape(PIECES, PROWS, WIDTH),
    )


def hand_over_kernel(student_ref, loss_ref, student_out, loss_out):
    student_out[...] = student_ref[...]
    loss_out[...] = loss_ref[...].reshape(ROWS)


def hand_over(student, loss):
    vmem = pl.BlockSpec(memory_space=pltpu.VMEM)
    return pl.pallas_call(
        hand_over_kernel,
        out_shape=(
            jax.ShapeDtypeStruct((ROWS, WIDTH), BF16),
            jax.ShapeDtypeStruct((ROWS,), F32),
        ),
        in_specs=[vmem, vmem],
        out_specs=(vmem, vmem),
        name="hand_over",
    )(student.reshape(ROWS, WIDTH), loss)


def body(*arguments):
    return hand_over(*block(*arguments))


def solution(mesh):
    in_specs = (
        P("ctx", "tp"),
        P("tp"),
        P(None, "tp"),
        P(None, "tp"),
        P(None, "tp"),
        P("tp", None),
        P(None, "tp"),
        P("ctx", "tp"),
    )
    out_specs = (P("ctx", "tp"), P("ctx"))
    return jax.shard_map(body, mesh=mesh, in_specs=in_specs, out_specs=out_specs, check_vma=False)
```

```python
import functools

import jax
import jax.numpy as jnp
from jax import lax
from jax.experimental import pallas as pl
from jax.experimental.pallas import tpu as pltpu
from jax.sharding import PartitionSpec as P

MESH = pl.DeviceIdType.MESH
F32 = jnp.float32
BF16 = jnp.bfloat16

D = 8192
QH = 32
HD = 128
ROWS = 512
TP = 16
WIDTH = D // TP
EPS_IN = 1e-05
EPS_OUT = 1e-06
CLIP_RATIO = 0.9
FAR_BELOW = -1e30
LOG2E = 1.4426950408889634
VMEM_LIMIT = 62 * 1024 * 1024


def tp_id(x, y, core):
    return lax.rem(x + 8, 4) * 4 + y * 2 + core


def tp_coords():
    me = lax.axis_index("tp")
    return me // 4, lax.rem(me // 2, 2), lax.rem(me, 2)


class Gather:
    def __init__(self, buf, send, recv):
        self.buf, self.send, self.recv = buf, send, recv
        x, y, core = tp_coords()
        self.core = core
        self.me = tp_id(x, y, core)
        self.right, self.left = tp_id(x + 1, y, core), tp_id(x - 1, y, core)
        self.across, self.mate = tp_id(x, 1 - y, core), tp_id(x, y, 1 - core)
        self.slots = [
            tp_id(x - 1, y, core),
            tp_id(x + 1, y, core),
            tp_id(x, 1 - y, core),
            tp_id(x + 2, y, core),
            tp_id(x - 1, 1 - y, core),
            tp_id(x + 1, 1 - y, core),
            tp_id(x + 2, 1 - y, core),
        ]
        self.mate_slots = [self.mate] + [s + 1 - 2 * core for s in self.slots]

    def slot_of(self, kind):
        return self.slots[kind] if kind < 7 else self.mate_slots[kind - 7]

    def copy(self, piece, kind, slot, target):
        return pltpu.make_async_remote_copy(
            src_ref=self.buf.at[piece, slot],
            dst_ref=self.buf.at[piece, slot],
            send_sem=self.send.at[piece, kind],
            recv_sem=self.recv.at[piece, kind],
            device_id={"tp": target},
            device_id_type=MESH,
        )

    def start_sideways(self, piece):
        self.copy(piece, 0, self.me, self.right).start()
        self.copy(piece, 1, self.me, self.left).start()

    def start_near(self, piece):
        self.copy(piece, 2, self.me, self.across).start()
        self.copy(piece, 7, self.me, self.mate).start()

    def landed(self, piece, kind):
        self.copy(piece, kind, self.slot_of(kind), self.mate).wait_recv()

    def forward(self, piece, kind, as_kind, target):
        self.copy(piece, as_kind, self.slots[kind], target).start()

    def from_sides(self, piece):
        self.landed(piece, 0)
        if piece % 2 == 0:
            self.forward(piece, 0, 3, self.right)
        self.forward(piece, 0, 8, self.mate)
        self.landed(piece, 1)
        if piece % 2 == 1:
            self.forward(piece, 1, 3, self.left)
        self.forward(piece, 1, 9, self.mate)

    def from_across(self, piece):
        self.landed(piece, 2)
        self.forward(piece, 2, 4, self.right)
        self.forward(piece, 2, 5, self.left)
        self.forward(piece, 2, 10, self.mate)

    def from_far(self, piece):
        self.landed(piece, 3)
        self.forward(piece, 3, 6, self.across)
        self.forward(piece, 3, 11, self.mate)

    def from_diagonal(self, piece):
        self.landed(piece, 4)
        self.forward(piece, 4, 12, self.mate)
        self.landed(piece, 5)
        self.forward(piece, 5, 13, self.mate)

    def from_far_across(self, piece):
        self.landed(piece, 6)
        self.forward(piece, 6, 14, self.mate)

    def mates_landed(self, piece, kinds):
        for kind in kinds:
            self.landed(piece, kind)

    def drain(self, pieces):
        def one(piece, carry):
            for kind in range(15):
                self.copy(piece, kind, self.me, self.mate).wait_send()
            return carry

        lax.fori_loop(0, pieces, one, 0)


def push_copy(j, box, send, recv, incoming=False):
    me = lax.axis_index("tp")
    slot = me ^ j if incoming else me
    return pltpu.make_async_remote_copy(
        src_ref=box.at[slot],
        dst_ref=box.at[slot],
        send_sem=send.at[j],
        recv_sem=recv.at[j],
        device_id={"tp": me ^ j},
        device_id_type=MESH,
    )


def push_start(box, send, recv):
    def one(j, carry):
        push_copy(j, box, send, recv).start()
        return carry

    lax.fori_loop(1, TP, one, 0)


def push_wait(box, send, recv):
    def one(j, carry):
        push_copy(j, box, send, recv, True).wait_recv()
        return carry

    lax.fori_loop(1, TP, one, 0)

    def sent(j, carry):
        push_copy(j, box, send, recv).wait_send()
        return carry

    lax.fori_loop(1, TP, sent, 0)


def to_lanes(column):
    n = column.shape[0]
    return jnp.transpose(jnp.broadcast_to(column, (n, 128)))[0:1, :]


def to_rows(lanes):
    n = lanes.shape[1]
    return jnp.transpose(jnp.broadcast_to(lanes, (128, n)))


PIECES = 4
PROWS = ROWS // PIECES
QROWS = 2 * ROWS
HALF = ROWS // 2
STRIP = 16


def pick(options, i):
    value = options[0]
    for n, option in enumerate(options[1:]):
        value = jnp.where(i == n + 1, option, value)
    return value


def block_kernel(
    x_hbm, gain_ref, wq_hbm, wk_hbm, wv_hbm, sign_ref, wo_hbm, teacher_hbm,
    student_hbm, loss_ref,
    xbuf, stats, wq, wkv, inv, accq, acckv, q, kvbuf, top, total, acc,
    sbuf, wo, rotated, branch, teacher, student, box1, box2,
    xsend, xrecv, ksend, krecv, ssend, srecv,
    psend0, precv0, psend1, precv1, psend2, precv2, wsend, wrecv, load_sem, x_sem,
):
    me = lax.axis_index("tp")
    ctx = lax.axis_index("ctx")
    rows = Gather(xbuf, xsend, xrecv)
    core, mate = rows.core, rows.mate

    x_loads = [
        pltpu.make_async_copy(x_hbm.at[p], xbuf.at[p, me], x_sem.at[p]) for p in range(PIECES)
    ]
    for load in x_loads:
        load.start()

    def half(base, whose):
        return pl.ds(pl.multiple_of(base + whose * 64, 64), 64)

    load_k = pltpu.make_async_copy(wk_hbm, wkv.at[half(0, core)], load_sem.at[0])
    load_v = pltpu.make_async_copy(wv_hbm, wkv.at[half(128, core)], load_sem.at[1])
    load_q = pltpu.make_async_copy(wq_hbm, wq, load_sem.at[2])
    load_o = pltpu.make_async_copy(wo_hbm, wo, load_sem.at[3])
    load_t = pltpu.make_async_copy(teacher_hbm, teacher, load_sem.at[4])
    load_k.start()
    load_v.start()
    load_q.start()

    row, z = ctx // 8, lax.rem(ctx, 8)
    sense = 1 - 2 * core
    other = (1 - row) * 8 + z

    def along(r, delta):
        return r * 8 + lax.rem(z + delta + 16, 8)

    to_ahead, to_behind = {"ctx": along(row, sense)}, {"ctx": along(row, -sense)}
    to_other, to_mate = {"ctx": other}, {"tp": mate}

    barrier = pltpu.get_barrier_semaphore()

    def greet(j, carry):
        pl.semaphore_signal(barrier, inc=1, device_id={"tp": me ^ j}, device_id_type=MESH)
        return carry

    lax.fori_loop(1, TP, greet, 0)
    for target in (to_ahead, to_behind, to_other):
        pl.semaphore_signal(barrier, inc=1, device_id=target, device_id_type=MESH)

    for p in range(PIECES):
        x_loads[p].wait()
        values = xbuf[p, me].astype(F32)
        stats[me, 0:1, p * PROWS : (p + 1) * PROWS] = to_lanes(
            jnp.sum(values * values, axis=1, keepdims=True)
        )
    stats[me, 1:2, :] = gain_ref[...].astype(F32).reshape(1, WIDTH)
    pl.semaphore_wait(barrier, TP - 1 + 3)

    push_start(stats, psend0, precv0)
    for p in range(PIECES):
        rows.start_sideways(p)
        rows.start_near(p)
    load_o.start()
    load_t.start()
    load_k.wait()
    load_v.wait()

    def share(base, whose, n):
        return pltpu.make_async_remote_copy(
            src_ref=wkv.at[half(base, whose)],
            dst_ref=wkv.at[half(base, whose)],
            send_sem=wsend.at[n],
            recv_sem=wrecv.at[n],
            device_id=to_mate,
            device_id_type=MESH,
        )

    share(0, core, 0).start()
    share(128, core, 1).start()
    push_wait(stats, psend0, precv0)
    squares = stats[0, 0:1, :]
    for slot in range(1, TP):
        squares = squares + stats[slot, 0:1, :]
    scale = lax.rsqrt(squares / D + EPS_IN)
    for p in range(PIECES):
        inv[p] = to_rows(scale[:, p * PROWS : (p + 1) * PROWS])
    accq[...] = jnp.zeros_like(accq)
    acckv[...] = jnp.zeros_like(acckv)

    load_q.wait()
    share(0, 1 - core, 0).wait_recv()
    share(128, 1 - core, 1).wait_recv()

    def consume(part, chip):
        at = pl.ds(pl.multiple_of(chip * 2 * WIDTH, 2 * WIDTH), 2 * WIDTH)
        both = []
        for slot in (2 * chip, 2 * chip + 1):
            gain = stats[slot, 1:2, :]
            for g in range(WIDTH // 128):
                lanes = slice(g * 128, (g + 1) * 128)
                column = []
                for p in (2 * part, 2 * part + 1):
                    values = xbuf[p, slot, :, lanes].astype(F32) * inv[p] * gain[:, lanes]
                    limit = CLIP_RATIO * jnp.max(jnp.abs(values), axis=-1, keepdims=True)
                    column.append(jnp.clip(values, -limit, limit).astype(BF16))
                both.append(jnp.concatenate(column, axis=0))
        quantized = jnp.concatenate(both, axis=1)
        accq[part] += jnp.dot(quantized, wq[at, :], preferred_element_type=F32)

        @pl.when(core == part)
        def _():
            acckv[...] += lax.dot_general(
                quantized, wkv[:, at], (((1,), (1,)), ((), ())), preferred_element_type=F32
            )

    def consume_all(part, kinds):
        chips = []
        for kind in kinds:
            for p in (2 * part, 2 * part + 1):
                rows.landed(p, 7 if kind is None else 8 + kind)
            chips.append((me if kind is None else rows.slots[kind]) // 2)

        def one(i, carry):
            consume(part, pick(chips, i))
            return carry

        lax.fori_loop(0, len(chips), one, 0)

    def kcopy(kind, block, part, target, g):
        return pltpu.make_async_remote_copy(
            src_ref=kvbuf.at[block, part, g],
            dst_ref=kvbuf.at[block, part, g],
            send_sem=ksend.at[g, kind],
            recv_sem=krecv.at[g, kind],
            device_id=target,
            device_id_type=MESH,
        )

    def klanded(kind, block, part, g):
        kcopy(kind, block, part, to_mate, g).wait_recv()

    def start_ring():
        for g in range(2):
            kcopy(0, ctx, core, to_ahead, g).start()
            kcopy(4, ctx, core, to_behind, g).start()
            kcopy(7, ctx, core, to_other, g).start()
            kcopy(15, ctx, core, to_mate, g).start()

    rings = {
        0: (0, -1, ((1, to_ahead), (8, to_other))),
        4: (0, 1, ((5, to_behind), (9, to_other))),
        1: (0, -2, ((2, to_ahead), (10, to_other))),
        5: (0, 2, ((6, to_behind), (11, to_other))),
        2: (0, -3, ((3, to_ahead),)),
        6: (0, 3, ()),
        3: (0, -4, ()),
        7: (1, 0, ()),
        8: (1, -1, ()),
        9: (1, 1, ()),
        10: (1, -2, ((12, to_ahead),)),
        11: (1, 2, ((14, to_behind),)),
        12: (1, -3, ((13, to_ahead),)),
        14: (1, 3, ()),
        13: (1, -4, ()),
    }

    def pass_on(*kinds):
        for g in range(2):
            for kind in kinds:
                far_row, delta, targets = rings[kind]
                block = along(1 - row if far_row else row, sense * delta)
                klanded(kind, block, core, g)
                for as_kind, target in targets:
                    kcopy(as_kind, block, core, target, g).start()
                kcopy(16 + kind, block, core, to_mate, g).start()

    rows.from_sides(0)
    rows.from_sides(1)
    rows.from_across(0)
    consume_all(0, (None,))
    rows.from_sides(2)
    rows.from_sides(3)
    rows.from_across(1)
    rows.from_across(2)
    rows.from_across(3)
    consume_all(1, (None,))
    consume_all(0, (0, 1))
    rows.from_far(0)
    rows.from_far(1)
    consume_all(0, (2,))
    rows.from_diagonal(0)
    consume_all(1, (0, 1))
    rows.from_far(2)
    rows.from_far(3)
    rows.from_far_across(0)
    consume_all(1, (2,))
    consume_all(0, (3,))
    rows.from_far_across(1)
    rows.from_diagonal(1)
    consume_all(1, (3,))
    consume_all(0, (4, 5, 6))
    rows.from_far_across(2)
    rows.from_diagonal(2)
    rows.from_far_across(3)
    rows.from_diagonal(3)
    consume_all(1, (4, 5, 6))
    kvbuf[ctx, core] = acckv[...].astype(BF16).reshape(2, PROWS, 2 * HD)
    for part in range(2):
        for head in range(2):
            q[head * ROWS + part * HALF : head * ROWS + (part + 1) * HALF, :] = accq[
                part, :, head * HD : (head + 1) * HD
            ].astype(BF16)
    start_ring()

    top[...] = jnp.full_like(top, FAR_BELOW)
    total[...] = jnp.zeros_like(total)
    acc[...] = jnp.zeros_like(acc)
    factor = HD ** (-0.5) * LOG2E

    def attend(keys, values, head, masked):
        at = slice(head * ROWS, (head + 1) * ROWS)
        scores = lax.dot_general(
            q[at, :], keys, (((1,), (1,)), ((), ())), preferred_element_type=F32
        )
        if masked:
            seen = lax.broadcasted_iota(jnp.int32, (ROWS, ROWS), 1) <= lax.broadcasted_iota(
                jnp.int32, (ROWS, ROWS), 0
            )
            scores = jnp.where(seen, scores, FAR_BELOW)
        high = jnp.max(scores, axis=-1, keepdims=True)
        before = top[at, :]
        now = jnp.maximum(before, jnp.broadcast_to(high, (ROWS, 128)))
        decay = jnp.exp2((before - now) * factor)
        shift = now * factor
        weights = []
        for g in range(ROWS // 128):
            lanes = slice(g * 128, (g + 1) * 128)
            part = jnp.exp2(scores[:, lanes] * factor - shift)
            if masked:
                part = jnp.where(seen[:, lanes], part, 0.0)
            weights.append(part)
        total[at, :] = decay * total[at, :] + ((weights[0] + weights[1]) + (weights[2] + weights[3]))
        mixed = jnp.dot(
            jnp.concatenate([part.astype(BF16) for part in weights], axis=1),
            values,
            preferred_element_type=F32,
        )
        acc[at, :] = decay * acc[at, :] + mixed
        top[at, :] = now

    def attend_block(block, masked):
        both = kvbuf[block].reshape(ROWS, 2 * HD)
        for head in range(2):
            attend(both[:, :HD], both[:, HD:], head, masked)

    order = (0, 4, 7, 1, 5, 8, 9, 2, 6, 10, 11, 3, 12, 14, 13)
    twin = {0: 4, 1: 5, 2: 6, 3: 3, 4: 0, 5: 1, 6: 2, 7: 7, 8: 9, 9: 8, 10: 11, 11: 10, 12: 14, 13: 13, 14: 12}

    def unit(j, carry):
        far_row = pick([jnp.int32(rings[kind][0]) for kind in order], j)
        delta = pick([jnp.int32(rings[kind][1]) for kind in order], j)
        kind = pick([jnp.int32(16 + twin[kind]) for kind in order], j)
        block = along(jnp.where(far_row == 1, 1 - row, row), sense * delta)
        for g in range(2):
            klanded(kind, block, 1 - core, g)

        @pl.when(block < ctx)
        def _():
            attend_block(block, False)

        return carry

    for g in range(2):
        klanded(15, ctx, 1 - core, g)
    attend_block(ctx, True)

    steps = ((0, 4), (7, 1, 5), (8, 9, 2, 6), (10, 11, 3), (12, 14), (13,))

    def ring_step(k, carry):
        for i, kinds in enumerate(steps):
            pl.when(k == i)(functools.partial(pass_on, *kinds))
        low = jnp.maximum(3 * k - 4, 0)
        high = jnp.minimum(jnp.maximum(3 * k - 1, 0), 15)
        lax.fori_loop(low, high, unit, 0)
        return carry

    lax.fori_loop(0, len(steps) + 1, ring_step, 0)

    heads = Gather(sbuf, ssend, srecv)
    for p in range(PIECES):
        for head in range(2):
            signs = (2 * sign_ref[head : head + 1, :] - 1).astype(F32)
            at = slice(head * ROWS + p * PROWS, head * ROWS + (p + 1) * PROWS)
            whole = jnp.sum(total[at, :], axis=-1, keepdims=True)
            attended = (acc[at, :] / whole).astype(BF16)
            sbuf[p, me, :, head * HD : (head + 1) * HD] = (
                attended.astype(F32) * signs
            ).astype(BF16)

    for p in range(PIECES):
        heads.start_sideways(p)
        heads.start_near(p)
    load_o.wait()
    load_t.wait()

    def rotate(p):
        heads.mates_landed(p, range(7, 15))

        def strip(i, carry):
            at = pl.ds(pl.multiple_of(i * STRIP, STRIP), STRIP)
            mix = []
            for slot in range(TP):
                both = sbuf[p, slot, at, :].astype(F32)
                mix += [both[:, :HD], both[:, HD:]]
            span = 1
            while span < QH:
                for h in range(QH):
                    if not h & span:
                        a, b = mix[h], mix[h + span]
                        mix[h], mix[h + span] = a + b, a - b
                span *= 2
            for h in range(QH):
                value = mix[h] * QH ** (-0.5)
                limit = CLIP_RATIO * jnp.max(jnp.abs(value), axis=-1, keepdims=True)
                rotated[p, at, h * HD : (h + 1) * HD] = jnp.clip(value, -limit, limit).astype(BF16)
            return carry

        lax.fori_loop(0, PROWS // STRIP, strip, 0)

    heads.from_sides(0)
    heads.from_sides(1)
    heads.from_across(0)
    heads.from_sides(2)
    heads.from_sides(3)
    heads.from_across(1)
    heads.from_across(2)
    heads.from_across(3)
    heads.from_far(0)
    heads.from_far(1)
    heads.from_diagonal(0)
    heads.from_far(2)
    heads.from_far(3)
    heads.from_diagonal(1)
    heads.from_far_across(0)
    rotate(0)
    heads.from_diagonal(2)
    heads.from_far_across(1)
    heads.from_diagonal(3)
    heads.from_far_across(2)
    rotate(1)
    heads.from_far_across(3)
    rotate(2)
    rotate(3)
    result = jnp.dot(
        rotated[...].reshape(ROWS, QH * HD), wo[...], preferred_element_type=F32
    )
    branch[...] = result.reshape(PIECES, PROWS, WIDTH)
    box1[me, 0:1, :] = to_lanes(jnp.sum(result * result, axis=1, keepdims=True))

    push_start(box1, psend1, precv1)
    rows.drain(PIECES)
    heads.drain(PIECES)
    share(0, core, 0).wait_send()
    share(128, core, 1).wait_send()

    def drain(kind, carry):
        for g in range(2):
            kcopy(kind, ctx, core, to_mate, g).wait_send()
        return carry

    lax.fori_loop(0, 31, drain, 0)
    push_wait(box1, psend1, precv1)
    squares = box1[0, 0:1, :]
    for slot in range(1, TP):
        squares = squares + box1[slot, 0:1, :]
    inverse = lax.rsqrt(squares / D + EPS_OUT)
    for p in range(PIECES):
        by_row = to_rows(inverse[:, p * PROWS : (p + 1) * PROWS])
        partial = jnp.zeros((PROWS, 128), F32)
        for g in range(WIDTH // 128):
            lanes = slice(g * 128, (g + 1) * 128)
            normal = branch[p, :, lanes] * by_row
            student[p, :, lanes] = normal.astype(BF16)
            difference = normal - teacher[p, :, lanes].astype(F32)
            partial = partial + difference * difference
        box2[me, 0:1, p * PROWS : (p + 1) * PROWS] = to_lanes(
            jnp.sum(partial, axis=1, keepdims=True)
        )
    push_start(box2, psend2, precv2)
    store = pltpu.make_async_copy(student, student_hbm, x_sem.at[0])
    store.start()
    push_wait(box2, psend2, precv2)
    loss = box2[0, 0:1, :]
    for slot in range(1, TP):
        loss = loss + box2[slot, 0:1, :]
    loss_ref[...] = loss / D
    store.wait()


def block(x, gain, w_query, w_key, w_value, sign_bits, w_out, teacher):
    any_space = pl.BlockSpec(memory_space=pl.ANY)
    vmem = pl.BlockSpec(memory_space=pltpu.VMEM)
    dma = pltpu.SemaphoreType.DMA
    return pl.pallas_call(
        block_kernel,
        out_shape=(
            jax.ShapeDtypeStruct((PIECES, PROWS, WIDTH), BF16),
            jax.ShapeDtypeStruct((1, ROWS), F32),
        ),
        in_specs=[any_space, vmem, any_space, any_space, any_space, vmem, any_space, any_space],
        out_specs=(any_space, vmem),
        scratch_shapes=[
            pltpu.VMEM((PIECES, TP, PROWS, WIDTH), BF16),
            pltpu.VMEM((TP, 2, ROWS), F32),
            pltpu.VMEM((D, 256), BF16),
            pltpu.VMEM((256, D), BF16),
            pltpu.VMEM((PIECES, PROWS, 128), F32),
            pltpu.VMEM((2, HALF, 256), F32),
            pltpu.VMEM((HALF, 256), F32),
            pltpu.VMEM((QROWS, HD), BF16),
            pltpu.VMEM((16, 2, 2, PROWS, 2 * HD), BF16),
            pltpu.VMEM((QROWS, 128), F32),
            pltpu.VMEM((QROWS, 128), F32),
            pltpu.VMEM((QROWS, HD), F32),
            pltpu.VMEM((PIECES, TP, PROWS, 2 * HD), BF16),
            pltpu.VMEM((QH * HD, WIDTH), BF16),
            pltpu.VMEM((PIECES, PROWS, QH * HD), BF16),
            pltpu.VMEM((PIECES, PROWS, WIDTH), F32),
            pltpu.VMEM((PIECES, PROWS, WIDTH), BF16),
            pltpu.VMEM((PIECES, PROWS, WIDTH), BF16),
            pltpu.VMEM((TP, 1, ROWS), F32),
            pltpu.VMEM((TP, 1, ROWS), F32),
            dma((PIECES, 15)),
            dma((PIECES, 15)),
            dma((2, 31)),
            dma((2, 31)),
            dma((PIECES, 15)),
            dma((PIECES, 15)),
            dma((TP,)),
            dma((TP,)),
            dma((TP,)),
            dma((TP,)),
            dma((TP,)),
            dma((TP,)),
            dma((2,)),
            dma((2,)),
            dma((5,)),
            dma((PIECES,)),
        ],
        compiler_params=pltpu.CompilerParams(
            collective_id=0, has_side_effects=True, vmem_limit_bytes=VMEM_LIMIT
        ),
        name="block",
    )(
        x.reshape(PIECES, PROWS, WIDTH),
        gain,
        w_query,
        w_key.T,
        w_value.T,
        sign_bits,
        w_out,
        teacher.reshape(PIECES, PROWS, WIDTH),
    )


def hand_over_kernel(student_ref, loss_ref, student_out, loss_out):
    student_out[...] = student_ref[...]
    loss_out[...] = loss_ref[...].reshape(ROWS)


def hand_over(student, loss):
    vmem = pl.BlockSpec(memory_space=pltpu.VMEM)
    return pl.pallas_call(
        hand_over_kernel,
        out_shape=(
            jax.ShapeDtypeStruct((ROWS, WIDTH), BF16),
            jax.ShapeDtypeStruct((ROWS,), F32),
        ),
        in_specs=[vmem, vmem],
        out_specs=(vmem, vmem),
        name="hand_over",
    )(student.reshape(ROWS, WIDTH), loss)


def body(*arguments):
    return hand_over(*block(*arguments))


def solution(mesh):
    in_specs = (
        P("ctx", "tp"),
        P("tp"),
        P(None, "tp"),
        P(None, "tp"),
        P(None, "tp"),
        P("tp", None),
        P(None, "tp"),
        P("ctx", "tp"),
    )
    out_specs = (P("ctx", "tp"), P("ctx"))
    return jax.shard_map(body, mesh=mesh, in_specs=in_specs, out_specs=out_specs, check_vma=False)
```

```python
import functools

import jax
import jax.numpy as jnp
from jax import lax
from jax.experimental import pallas as pl
from jax.experimental.pallas import tpu as pltpu
from jax.sharding import PartitionSpec as P

MESH = pl.DeviceIdType.MESH
F32 = jnp.float32
BF16 = jnp.bfloat16

D = 8192
QH = 32
HD = 128
ROWS = 512
TP = 16
WIDTH = D // TP
EPS_IN = 1e-05
EPS_OUT = 1e-06
CLIP_RATIO = 0.9
FAR_BELOW = -1e30
LOG2E = 1.4426950408889634
VMEM_LIMIT = 62 * 1024 * 1024


def tp_id(x, y, core):
    return lax.rem(x + 8, 4) * 4 + y * 2 + core


def tp_coords():
    me = lax.axis_index("tp")
    return me // 4, lax.rem(me // 2, 2), lax.rem(me, 2)


class Gather:
    def __init__(self, buf, send, recv):
        self.buf, self.send, self.recv = buf, send, recv
        x, y, core = tp_coords()
        self.core = core
        self.me = tp_id(x, y, core)
        self.right, self.left = tp_id(x + 1, y, core), tp_id(x - 1, y, core)
        self.across, self.mate = tp_id(x, 1 - y, core), tp_id(x, y, 1 - core)
        self.slots = [
            tp_id(x - 1, y, core),
            tp_id(x + 1, y, core),
            tp_id(x, 1 - y, core),
            tp_id(x + 2, y, core),
            tp_id(x - 1, 1 - y, core),
            tp_id(x + 1, 1 - y, core),
            tp_id(x + 2, 1 - y, core),
        ]
        self.mate_slots = [self.mate] + [s + 1 - 2 * core for s in self.slots]

    def slot_of(self, kind):
        return self.slots[kind] if kind < 7 else self.mate_slots[kind - 7]

    def copy(self, piece, kind, slot, target):
        return pltpu.make_async_remote_copy(
            src_ref=self.buf.at[piece, slot],
            dst_ref=self.buf.at[piece, slot],
            send_sem=self.send.at[piece, kind],
            recv_sem=self.recv.at[piece, kind],
            device_id={"tp": target},
            device_id_type=MESH,
        )

    def start_sideways(self, piece):
        self.copy(piece, 0, self.me, self.right).start()
        self.copy(piece, 1, self.me, self.left).start()

    def start_near(self, piece):
        self.copy(piece, 2, self.me, self.across).start()
        self.copy(piece, 7, self.me, self.mate).start()

    def landed(self, piece, kind):
        self.copy(piece, kind, self.slot_of(kind), self.mate).wait_recv()

    def forward(self, piece, kind, as_kind, target):
        self.copy(piece, as_kind, self.slots[kind], target).start()

    def from_sides(self, piece):
        self.landed(piece, 0)
        if piece % 2 == 0:
            self.forward(piece, 0, 3, self.right)
        self.forward(piece, 0, 8, self.mate)
        self.landed(piece, 1)
        if piece % 2 == 1:
            self.forward(piece, 1, 3, self.left)
        self.forward(piece, 1, 9, self.mate)

    def from_across(self, piece):
        self.landed(piece, 2)
        self.forward(piece, 2, 4, self.right)
        self.forward(piece, 2, 5, self.left)
        self.forward(piece, 2, 10, self.mate)

    def from_far(self, piece):
        self.landed(piece, 3)
        self.forward(piece, 3, 6, self.across)
        self.forward(piece, 3, 11, self.mate)

    def from_diagonal(self, piece):
        self.landed(piece, 4)
        self.forward(piece, 4, 12, self.mate)
        self.landed(piece, 5)
        self.forward(piece, 5, 13, self.mate)

    def from_far_across(self, piece):
        self.landed(piece, 6)
        self.forward(piece, 6, 14, self.mate)

    def mates_landed(self, piece, kinds):
        for kind in kinds:
            self.landed(piece, kind)

    def drain(self, pieces):
        def one(piece, carry):
            for kind in range(15):
                self.copy(piece, kind, self.me, self.mate).wait_send()
            return carry

        lax.fori_loop(0, pieces, one, 0)


def push_copy(j, box, send, recv, incoming=False):
    me = lax.axis_index("tp")
    slot = me ^ j if incoming else me
    return pltpu.make_async_remote_copy(
        src_ref=box.at[slot],
        dst_ref=box.at[slot],
        send_sem=send.at[j],
        recv_sem=recv.at[j],
        device_id={"tp": me ^ j},
        device_id_type=MESH,
    )


def push_start(box, send, recv):
    def one(j, carry):
        push_copy(j, box, send, recv).start()
        return carry

    lax.fori_loop(1, TP, one, 0)


def push_wait(box, send, recv):
    def one(j, carry):
        push_copy(j, box, send, recv, True).wait_recv()
        return carry

    lax.fori_loop(1, TP, one, 0)

    def sent(j, carry):
        push_copy(j, box, send, recv).wait_send()
        return carry

    lax.fori_loop(1, TP, sent, 0)


def to_lanes(column):
    n = column.shape[0]
    return jnp.transpose(jnp.broadcast_to(column, (n, 128)))[0:1, :]


def to_rows(lanes):
    n = lanes.shape[1]
    return jnp.transpose(jnp.broadcast_to(lanes, (128, n)))


PIECES = 4
PROWS = ROWS // PIECES
QROWS = 2 * ROWS
HALF = ROWS // 2
STRIP = 16


def pick(options, i):
    value = options[0]
    for n, option in enumerate(options[1:]):
        value = jnp.where(i == n + 1, option, value)
    return value


def block_kernel(
    x_hbm, gain_ref, wq_hbm, wk_hbm, wv_hbm, sign_ref, wo_hbm, teacher_hbm,
    student_hbm, loss_ref,
    xbuf, stats, wq, wkv, inv, accq, acckv, q, kvbuf, top, total, acc,
    sbuf, wo, rotated, branch, teacher, student, box1, box2,
    xsend, xrecv, ksend, krecv, ssend, srecv,
    psend0, precv0, psend1, precv1, psend2, precv2, wsend, wrecv, load_sem, x_sem,
):
    me = lax.axis_index("tp")
    ctx = lax.axis_index("ctx")
    rows = Gather(xbuf, xsend, xrecv)
    core, mate = rows.core, rows.mate

    x_loads = [
        pltpu.make_async_copy(x_hbm.at[p], xbuf.at[p, me], x_sem.at[p]) for p in range(PIECES)
    ]
    for load in x_loads:
        load.start()

    def half(base, whose):
        return pl.ds(pl.multiple_of(base + whose * 64, 64), 64)

    load_k = pltpu.make_async_copy(wk_hbm, wkv.at[half(0, core)], load_sem.at[0])
    load_v = pltpu.make_async_copy(wv_hbm, wkv.at[half(128, core)], load_sem.at[1])
    load_q = pltpu.make_async_copy(wq_hbm, wq, load_sem.at[2])
    load_o = pltpu.make_async_copy(wo_hbm, wo, load_sem.at[3])
    load_t = pltpu.make_async_copy(teacher_hbm, teacher, load_sem.at[4])
    load_k.start()
    load_v.start()
    load_q.start()

    row, z = ctx // 8, lax.rem(ctx, 8)
    sense = 1 - 2 * core
    other = (1 - row) * 8 + z

    def along(r, delta):
        return r * 8 + lax.rem(z + delta + 16, 8)

    to_ahead, to_behind = {"ctx": along(row, sense)}, {"ctx": along(row, -sense)}
    to_other, to_mate = {"ctx": other}, {"tp": mate}

    barrier = pltpu.get_barrier_semaphore()

    def greet(j, carry):
        pl.semaphore_signal(barrier, inc=1, device_id={"tp": me ^ j}, device_id_type=MESH)
        return carry

    lax.fori_loop(1, TP, greet, 0)
    for target in (to_ahead, to_behind, to_other):
        pl.semaphore_signal(barrier, inc=1, device_id=target, device_id_type=MESH)

    for p in range(PIECES):
        x_loads[p].wait()
        values = xbuf[p, me].astype(F32)
        stats[me, 0:1, p * PROWS : (p + 1) * PROWS] = to_lanes(
            jnp.sum(values * values, axis=1, keepdims=True)
        )
    stats[me, 1:2, :] = gain_ref[...].astype(F32).reshape(1, WIDTH)
    pl.semaphore_wait(barrier, TP - 1 + 3)

    push_start(stats, psend0, precv0)
    for p in range(PIECES):
        rows.start_sideways(p)
        rows.start_near(p)
    load_o.start()
    load_t.start()
    load_k.wait()
    load_v.wait()

    def share(base, whose, n):
        return pltpu.make_async_remote_copy(
            src_ref=wkv.at[half(base, whose)],
            dst_ref=wkv.at[half(base, whose)],
            send_sem=wsend.at[n],
            recv_sem=wrecv.at[n],
            device_id=to_mate,
            device_id_type=MESH,
        )

    share(0, core, 0).start()
    share(128, core, 1).start()
    push_wait(stats, psend0, precv0)
    squares = stats[0, 0:1, :]
    for slot in range(1, TP):
        squares = squares + stats[slot, 0:1, :]
    scale = lax.rsqrt(squares / D + EPS_IN)
    for p in range(PIECES):
        inv[p] = to_rows(scale[:, p * PROWS : (p + 1) * PROWS])
    accq[...] = jnp.zeros_like(accq)
    acckv[...] = jnp.zeros_like(acckv)

    load_q.wait()
    share(0, 1 - core, 0).wait_recv()
    share(128, 1 - core, 1).wait_recv()

    def consume(part, chip):
        at = pl.ds(pl.multiple_of(chip * 2 * WIDTH, 2 * WIDTH), 2 * WIDTH)
        both = []
        for slot in (2 * chip, 2 * chip + 1):
            gain = stats[slot, 1:2, :]
            for g in range(WIDTH // 128):
                lanes = slice(g * 128, (g + 1) * 128)
                column = []
                for p in (2 * part, 2 * part + 1):
                    values = xbuf[p, slot, :, lanes].astype(F32) * inv[p] * gain[:, lanes]
                    limit = CLIP_RATIO * jnp.max(jnp.abs(values), axis=-1, keepdims=True)
                    column.append(jnp.clip(values, -limit, limit).astype(BF16))
                both.append(jnp.concatenate(column, axis=0))
        quantized = jnp.concatenate(both, axis=1)
        accq[part] += jnp.dot(quantized, wq[at, :], preferred_element_type=F32)

        @pl.when(core == part)
        def _():
            acckv[...] += lax.dot_general(
                quantized, wkv[:, at], (((1,), (1,)), ((), ())), preferred_element_type=F32
            )

    def consume_all(part, kinds):
        chips = []
        for kind in kinds:
            for p in (2 * part, 2 * part + 1):
                rows.landed(p, 7 if kind is None else 8 + kind)
            chips.append((me if kind is None else rows.slots[kind]) // 2)

        def one(i, carry):
            consume(part, pick(chips, i))
            return carry

        lax.fori_loop(0, len(chips), one, 0)

    def kcopy(kind, block, part, target, g):
        return pltpu.make_async_remote_copy(
            src_ref=kvbuf.at[block, part, g],
            dst_ref=kvbuf.at[block, part, g],
            send_sem=ksend.at[g, kind],
            recv_sem=krecv.at[g, kind],
            device_id=target,
            device_id_type=MESH,
        )

    def klanded(kind, block, part, g):
        kcopy(kind, block, part, to_mate, g).wait_recv()

    def start_ring():
        for g in range(2):
            kcopy(0, ctx, core, to_ahead, g).start()
            kcopy(4, ctx, core, to_behind, g).start()
            kcopy(7, ctx, core, to_other, g).start()
            kcopy(15, ctx, core, to_mate, g).start()

    rings = {
        0: (0, -1, ((1, to_ahead), (8, to_other))),
        4: (0, 1, ((5, to_behind), (9, to_other))),
        1: (0, -2, ((2, to_ahead), (10, to_other))),
        5: (0, 2, ((6, to_behind), (11, to_other))),
        2: (0, -3, ((3, to_ahead),)),
        6: (0, 3, ()),
        3: (0, -4, ()),
        7: (1, 0, ()),
        8: (1, -1, ()),
        9: (1, 1, ()),
        10: (1, -2, ((12, to_ahead),)),
        11: (1, 2, ((14, to_behind),)),
        12: (1, -3, ((13, to_ahead),)),
        14: (1, 3, ()),
        13: (1, -4, ()),
    }

    def pass_on(*kinds):
        for g in range(2):
            for kind in kinds:
                far_row, delta, targets = rings[kind]
                block = along(1 - row if far_row else row, sense * delta)
                klanded(kind, block, core, g)
                for as_kind, target in targets:
                    kcopy(as_kind, block, core, target, g).start()
                kcopy(16 + kind, block, core, to_mate, g).start()

    rows.from_sides(0)
    rows.from_sides(1)
    rows.from_across(0)
    consume_all(0, (None,))
    rows.from_sides(2)
    rows.from_sides(3)
    rows.from_across(1)
    rows.from_across(2)
    rows.from_across(3)
    consume_all(1, (None,))
    consume_all(0, (0, 1))
    rows.from_far(0)
    rows.from_far(1)
    consume_all(0, (2,))
    rows.from_diagonal(0)
    consume_all(1, (0, 1))
    rows.from_far(2)
    rows.from_far(3)
    rows.from_far_across(0)
    consume_all(1, (2,))
    consume_all(0, (3,))
    rows.from_far_across(1)
    rows.from_diagonal(1)
    consume_all(1, (3,))
    consume_all(0, (4, 5, 6))

    def keep_kv():
        kvbuf[ctx, core] = acckv[...].astype(BF16).reshape(2, PROWS, 2 * HD)

    pl.when(core == 0)(keep_kv)
    rows.from_far_across(2)
    rows.from_diagonal(2)
    pl.when(core == 0)(start_ring)
    rows.from_far_across(3)
    consume_all(1, (6,))
    rows.from_diagonal(3)
    consume_all(1, (4, 5))
    pl.when(core == 1)(keep_kv)
    for part in range(2):
        for head in range(2):
            q[head * ROWS + part * HALF : head * ROWS + (part + 1) * HALF, :] = accq[
                part, :, head * HD : (head + 1) * HD
            ].astype(BF16)
    pl.when(core == 1)(start_ring)
    pl.when(core == 0)(functools.partial(pass_on, 0, 4))

    top[...] = jnp.full_like(top, FAR_BELOW)
    total[...] = jnp.zeros_like(total)
    acc[...] = jnp.zeros_like(acc)
    factor = HD ** (-0.5) * LOG2E

    def attend(keys, values, head, masked):
        at = slice(head * ROWS, (head + 1) * ROWS)
        scores = lax.dot_general(
            q[at, :], keys, (((1,), (1,)), ((), ())), preferred_element_type=F32
        )
        if masked:
            seen = lax.broadcasted_iota(jnp.int32, (ROWS, ROWS), 1) <= lax.broadcasted_iota(
                jnp.int32, (ROWS, ROWS), 0
            )
            scores = jnp.where(seen, scores, FAR_BELOW)
        high = jnp.max(scores, axis=-1, keepdims=True)
        before = top[at, :]
        now = jnp.maximum(before, jnp.broadcast_to(high, (ROWS, 128)))
        decay = jnp.exp2((before - now) * factor)
        shift = now * factor
        weights = []
        for g in range(ROWS // 128):
            lanes = slice(g * 128, (g + 1) * 128)
            part = jnp.exp2(scores[:, lanes] * factor - shift)
            if masked:
                part = jnp.where(seen[:, lanes], part, 0.0)
            weights.append(part)
        total[at, :] = decay * total[at, :] + ((weights[0] + weights[1]) + (weights[2] + weights[3]))
        mixed = jnp.dot(
            jnp.concatenate([part.astype(BF16) for part in weights], axis=1),
            values,
            preferred_element_type=F32,
        )
        acc[at, :] = decay * acc[at, :] + mixed
        top[at, :] = now

    def attend_block(block, masked):
        both = kvbuf[block].reshape(ROWS, 2 * HD)
        for head in range(2):
            attend(both[:, :HD], both[:, HD:], head, masked)

    order = (0, 4, 7, 1, 5, 8, 9, 2, 6, 10, 11, 3, 12, 14, 13)
    twin = {0: 4, 1: 5, 2: 6, 3: 3, 4: 0, 5: 1, 6: 2, 7: 7, 8: 9, 9: 8, 10: 11, 11: 10, 12: 14, 13: 13, 14: 12}

    def unit(j, carry):
        far_row = pick([jnp.int32(rings[kind][0]) for kind in order], j)
        delta = pick([jnp.int32(rings[kind][1]) for kind in order], j)
        kind = pick([jnp.int32(16 + twin[kind]) for kind in order], j)
        block = along(jnp.where(far_row == 1, 1 - row, row), sense * delta)
        for g in range(2):
            klanded(kind, block, 1 - core, g)

        @pl.when(block < ctx)
        def _():
            attend_block(block, False)

        return carry

    for g in range(2):
        klanded(15, ctx, 1 - core, g)
    attend_block(ctx, True)

    steps = ((0, 4), (7, 1, 5), (8, 9, 2, 6), (10, 11, 3), (12, 14), (13,))

    def ring_step(k, carry):
        for i, kinds in enumerate(steps):
            now = (k == i) & (core == 1) if i == 0 else k == i
            pl.when(now)(functools.partial(pass_on, *kinds))
        low = jnp.maximum(3 * k - 4, 0)
        high = jnp.minimum(jnp.maximum(3 * k - 1, 0), 15)
        lax.fori_loop(low, high, unit, 0)
        return carry

    lax.fori_loop(0, len(steps) + 1, ring_step, 0)

    heads = Gather(sbuf, ssend, srecv)
    for p in range(PIECES):
        for head in range(2):
            signs = (2 * sign_ref[head : head + 1, :] - 1).astype(F32)
            at = slice(head * ROWS + p * PROWS, head * ROWS + (p + 1) * PROWS)
            whole = jnp.sum(total[at, :], axis=-1, keepdims=True)
            attended = (acc[at, :] / whole).astype(BF16)
            sbuf[p, me, :, head * HD : (head + 1) * HD] = (
                attended.astype(F32) * signs
            ).astype(BF16)

    for p in range(PIECES):
        heads.start_sideways(p)
        heads.start_near(p)
    load_o.wait()
    load_t.wait()

    def rotate(p):
        heads.mates_landed(p, range(7, 15))

        def strip(i, carry):
            at = pl.ds(pl.multiple_of(i * STRIP, STRIP), STRIP)
            mix = []
            for slot in range(TP):
                both = sbuf[p, slot, at, :].astype(F32)
                mix += [both[:, :HD], both[:, HD:]]
            span = 1
            while span < QH:
                for h in range(QH):
                    if not h & span:
                        a, b = mix[h], mix[h + span]
                        mix[h], mix[h + span] = a + b, a - b
                span *= 2
            for h in range(QH):
                value = mix[h] * QH ** (-0.5)
                limit = CLIP_RATIO * jnp.max(jnp.abs(value), axis=-1, keepdims=True)
                rotated[p, at, h * HD : (h + 1) * HD] = jnp.clip(value, -limit, limit).astype(BF16)
            return carry

        lax.fori_loop(0, PROWS // STRIP, strip, 0)

    heads.from_sides(0)
    heads.from_sides(1)
    heads.from_across(0)
    heads.from_sides(2)
    heads.from_sides(3)
    heads.from_across(1)
    heads.from_across(2)
    heads.from_across(3)
    heads.from_far(0)
    heads.from_far(1)
    heads.from_diagonal(0)
    heads.from_far(2)
    heads.from_far(3)
    heads.from_diagonal(1)
    heads.from_far_across(0)
    rotate(0)
    heads.from_diagonal(2)
    heads.from_far_across(1)
    heads.from_diagonal(3)
    heads.from_far_across(2)
    rotate(1)
    heads.from_far_across(3)
    rotate(2)
    rotate(3)
    result = jnp.dot(
        rotated[...].reshape(ROWS, QH * HD), wo[...], preferred_element_type=F32
    )
    branch[...] = result.reshape(PIECES, PROWS, WIDTH)
    box1[me, 0:1, :] = to_lanes(jnp.sum(result * result, axis=1, keepdims=True))

    push_start(box1, psend1, precv1)
    rows.drain(PIECES)
    heads.drain(PIECES)
    share(0, core, 0).wait_send()
    share(128, core, 1).wait_send()

    def drain(kind, carry):
        for g in range(2):
            kcopy(kind, ctx, core, to_mate, g).wait_send()
        return carry

    lax.fori_loop(0, 31, drain, 0)
    push_wait(box1, psend1, precv1)
    squares = box1[0, 0:1, :]
    for slot in range(1, TP):
        squares = squares + box1[slot, 0:1, :]
    inverse = lax.rsqrt(squares / D + EPS_OUT)
    for p in range(PIECES):
        by_row = to_rows(inverse[:, p * PROWS : (p + 1) * PROWS])
        partial = jnp.zeros((PROWS, 128), F32)
        for g in range(WIDTH // 128):
            lanes = slice(g * 128, (g + 1) * 128)
            normal = branch[p, :, lanes] * by_row
            student[p, :, lanes] = normal.astype(BF16)
            difference = normal - teacher[p, :, lanes].astype(F32)
            partial = partial + difference * difference
        box2[me, 0:1, p * PROWS : (p + 1) * PROWS] = to_lanes(
            jnp.sum(partial, axis=1, keepdims=True)
        )
    push_start(box2, psend2, precv2)
    store = pltpu.make_async_copy(student, student_hbm, x_sem.at[0])
    store.start()
    push_wait(box2, psend2, precv2)
    loss = box2[0, 0:1, :]
    for slot in range(1, TP):
        loss = loss + box2[slot, 0:1, :]
    loss_ref[...] = loss / D
    store.wait()


def block(x, gain, w_query, w_key, w_value, sign_bits, w_out, teacher):
    any_space = pl.BlockSpec(memory_space=pl.ANY)
    vmem = pl.BlockSpec(memory_space=pltpu.VMEM)
    dma = pltpu.SemaphoreType.DMA
    return pl.pallas_call(
        block_kernel,
        out_shape=(
            jax.ShapeDtypeStruct((PIECES, PROWS, WIDTH), BF16),
            jax.ShapeDtypeStruct((1, ROWS), F32),
        ),
        in_specs=[any_space, vmem, any_space, any_space, any_space, vmem, any_space, any_space],
        out_specs=(any_space, vmem),
        scratch_shapes=[
            pltpu.VMEM((PIECES, TP, PROWS, WIDTH), BF16),
            pltpu.VMEM((TP, 2, ROWS), F32),
            pltpu.VMEM((D, 256), BF16),
            pltpu.VMEM((256, D), BF16),
            pltpu.VMEM((PIECES, PROWS, 128), F32),
            pltpu.VMEM((2, HALF, 256), F32),
            pltpu.VMEM((HALF, 256), F32),
            pltpu.VMEM((QROWS, HD), BF16),
            pltpu.VMEM((16, 2, 2, PROWS, 2 * HD), BF16),
            pltpu.VMEM((QROWS, 128), F32),
            pltpu.VMEM((QROWS, 128), F32),
            pltpu.VMEM((QROWS, HD), F32),
            pltpu.VMEM((PIECES, TP, PROWS, 2 * HD), BF16),
            pltpu.VMEM((QH * HD, WIDTH), BF16),
            pltpu.VMEM((PIECES, PROWS, QH * HD), BF16),
            pltpu.VMEM((PIECES, PROWS, WIDTH), F32),
            pltpu.VMEM((PIECES, PROWS, WIDTH), BF16),
            pltpu.VMEM((PIECES, PROWS, WIDTH), BF16),
            pltpu.VMEM((TP, 1, ROWS), F32),
            pltpu.VMEM((TP, 1, ROWS), F32),
            dma((PIECES, 15)),
            dma((PIECES, 15)),
            dma((2, 31)),
            dma((2, 31)),
            dma((PIECES, 15)),
            dma((PIECES, 15)),
            dma((TP,)),
            dma((TP,)),
            dma((TP,)),
            dma((TP,)),
            dma((TP,)),
            dma((TP,)),
            dma((2,)),
            dma((2,)),
            dma((5,)),
            dma((PIECES,)),
        ],
        compiler_params=pltpu.CompilerParams(
            collective_id=0, has_side_effects=True, vmem_limit_bytes=VMEM_LIMIT
        ),
        name="block",
    )(
        x.reshape(PIECES, PROWS, WIDTH),
        gain,
        w_query,
        w_key.T,
        w_value.T,
        sign_bits,
        w_out,
        teacher.reshape(PIECES, PROWS, WIDTH),
    )


def hand_over_kernel(student_ref, loss_ref, student_out, loss_out):
    student_out[...] = student_ref[...]
    loss_out[...] = loss_ref[...].reshape(ROWS)


def hand_over(student, loss):
    vmem = pl.BlockSpec(memory_space=pltpu.VMEM)
    return pl.pallas_call(
        hand_over_kernel,
        out_shape=(
            jax.ShapeDtypeStruct((ROWS, WIDTH), BF16),
            jax.ShapeDtypeStruct((ROWS,), F32),
        ),
        in_specs=[vmem, vmem],
        out_specs=(vmem, vmem),
        name="hand_over",
    )(student.reshape(ROWS, WIDTH), loss)


def body(*arguments):
    return hand_over(*block(*arguments))


def solution(mesh):
    in_specs = (
        P("ctx", "tp"),
        P("tp"),
        P(None, "tp"),
        P(None, "tp"),
        P(None, "tp"),
        P("tp", None),
        P(None, "tp"),
        P("ctx", "tp"),
    )
    out_specs = (P("ctx", "tp"), P("ctx"))
    return jax.shard_map(body, mesh=mesh, in_specs=in_specs, out_specs=out_specs, check_vma=False)
```

```python
import functools

import jax
import jax.numpy as jnp
from jax import lax
from jax.experimental import pallas as pl
from jax.experimental.pallas import tpu as pltpu
from jax.sharding import PartitionSpec as P

MESH = pl.DeviceIdType.MESH
F32 = jnp.float32
BF16 = jnp.bfloat16

D = 8192
QH = 32
HD = 128
ROWS = 512
TP = 16
WIDTH = D // TP
EPS_IN = 1e-05
EPS_OUT = 1e-06
CLIP_RATIO = 0.9
FAR_BELOW = -1e30
LOG2E = 1.4426950408889634
VMEM_LIMIT = 62 * 1024 * 1024


def tp_id(x, y, core):
    return lax.rem(x + 8, 4) * 4 + y * 2 + core


def tp_coords():
    me = lax.axis_index("tp")
    return me // 4, lax.rem(me // 2, 2), lax.rem(me, 2)


class Gather:
    def __init__(self, buf, send, recv):
        self.buf, self.send, self.recv = buf, send, recv
        x, y, core = tp_coords()
        self.core = core
        self.me = tp_id(x, y, core)
        self.right, self.left = tp_id(x + 1, y, core), tp_id(x - 1, y, core)
        self.across, self.mate = tp_id(x, 1 - y, core), tp_id(x, y, 1 - core)
        self.slots = [
            tp_id(x - 1, y, core),
            tp_id(x + 1, y, core),
            tp_id(x, 1 - y, core),
            tp_id(x + 2, y, core),
            tp_id(x - 1, 1 - y, core),
            tp_id(x + 1, 1 - y, core),
            tp_id(x + 2, 1 - y, core),
        ]
        self.mate_slots = [self.mate] + [s + 1 - 2 * core for s in self.slots]

    def slot_of(self, kind):
        return self.slots[kind] if kind < 7 else self.mate_slots[kind - 7]

    def copy(self, piece, kind, slot, target):
        return pltpu.make_async_remote_copy(
            src_ref=self.buf.at[piece, slot],
            dst_ref=self.buf.at[piece, slot],
            send_sem=self.send.at[piece, kind],
            recv_sem=self.recv.at[piece, kind],
            device_id={"tp": target},
            device_id_type=MESH,
        )

    def start_sideways(self, piece):
        self.copy(piece, 0, self.me, self.right).start()
        self.copy(piece, 1, self.me, self.left).start()

    def start_near(self, piece):
        self.copy(piece, 2, self.me, self.across).start()
        self.copy(piece, 7, self.me, self.mate).start()

    def landed(self, piece, kind):
        self.copy(piece, kind, self.slot_of(kind), self.mate).wait_recv()

    def forward(self, piece, kind, as_kind, target):
        self.copy(piece, as_kind, self.slots[kind], target).start()

    def from_sides(self, piece):
        self.landed(piece, 0)
        if piece % 2 == 0:
            self.forward(piece, 0, 3, self.right)
        self.forward(piece, 0, 8, self.mate)
        self.landed(piece, 1)
        if piece % 2 == 1:
            self.forward(piece, 1, 3, self.left)
        self.forward(piece, 1, 9, self.mate)

    def from_across(self, piece):
        self.landed(piece, 2)
        self.forward(piece, 2, 4, self.right)
        self.forward(piece, 2, 5, self.left)
        self.forward(piece, 2, 10, self.mate)

    def from_far(self, piece):
        self.landed(piece, 3)
        self.forward(piece, 3, 6, self.across)
        self.forward(piece, 3, 11, self.mate)

    def from_diagonal(self, piece):
        self.landed(piece, 4)
        self.forward(piece, 4, 12, self.mate)
        self.landed(piece, 5)
        self.forward(piece, 5, 13, self.mate)

    def from_far_across(self, piece):
        self.landed(piece, 6)
        self.forward(piece, 6, 14, self.mate)

    def mates_landed(self, piece, kinds):
        for kind in kinds:
            self.landed(piece, kind)

    def drain(self, pieces):
        def one(piece, carry):
            for kind in range(15):
                self.copy(piece, kind, self.me, self.mate).wait_send()
            return carry

        lax.fori_loop(0, pieces, one, 0)


def push_copy(j, box, send, recv, incoming=False):
    me = lax.axis_index("tp")
    slot = me ^ j if incoming else me
    return pltpu.make_async_remote_copy(
        src_ref=box.at[slot],
        dst_ref=box.at[slot],
        send_sem=send.at[j],
        recv_sem=recv.at[j],
        device_id={"tp": me ^ j},
        device_id_type=MESH,
    )


def push_start(box, send, recv):
    def one(j, carry):
        push_copy(j, box, send, recv).start()
        return carry

    lax.fori_loop(1, TP, one, 0)


def push_wait(box, send, recv):
    def one(j, carry):
        push_copy(j, box, send, recv, True).wait_recv()
        return carry

    lax.fori_loop(1, TP, one, 0)

    def sent(j, carry):
        push_copy(j, box, send, recv).wait_send()
        return carry

    lax.fori_loop(1, TP, sent, 0)


def to_lanes(column):
    n = column.shape[0]
    return jnp.transpose(jnp.broadcast_to(column, (n, 128)))[0:1, :]


def to_rows(lanes):
    n = lanes.shape[1]
    return jnp.transpose(jnp.broadcast_to(lanes, (128, n)))


PIECES = 4
PROWS = ROWS // PIECES
QROWS = 2 * ROWS
HALF = ROWS // 2
STRIP = 16


def pick(options, i):
    value = options[0]
    for n, option in enumerate(options[1:]):
        value = jnp.where(i == n + 1, option, value)
    return value


def block_kernel(
    x_hbm, gain_ref, wq_hbm, wk_hbm, wv_hbm, sign_ref, wo_hbm, teacher_hbm,
    student_hbm, loss_ref,
    xbuf, stats, wq, wkv, inv, accq, acckv, q, kvbuf, top, total, acc,
    sbuf, wo, rotated, branch, teacher, student, box1, box2,
    xsend, xrecv, ksend, krecv, ssend, srecv,
    psend0, precv0, psend1, precv1, psend2, precv2, wsend, wrecv, load_sem, x_sem,
):
    me = lax.axis_index("tp")
    ctx = lax.axis_index("ctx")
    rows = Gather(xbuf, xsend, xrecv)
    core, mate = rows.core, rows.mate

    x_loads = [
        pltpu.make_async_copy(x_hbm.at[p], xbuf.at[p, me], x_sem.at[p]) for p in range(PIECES)
    ]
    for load in x_loads:
        load.start()

    def half(base, whose):
        return pl.ds(pl.multiple_of(base + whose * 64, 64), 64)

    load_k = pltpu.make_async_copy(wk_hbm, wkv.at[half(0, core)], load_sem.at[0])
    load_v = pltpu.make_async_copy(wv_hbm, wkv.at[half(128, core)], load_sem.at[1])
    load_q = pltpu.make_async_copy(wq_hbm, wq, load_sem.at[2])
    load_o = pltpu.make_async_copy(wo_hbm, wo, load_sem.at[3])
    load_t = pltpu.make_async_copy(teacher_hbm, teacher, load_sem.at[4])
    load_k.start()
    load_v.start()
    load_q.start()

    row, z = ctx // 8, lax.rem(ctx, 8)
    sense = 1 - 2 * core
    other = (1 - row) * 8 + z

    def along(r, delta):
        return r * 8 + lax.rem(z + delta + 16, 8)

    to_ahead, to_behind = {"ctx": along(row, sense)}, {"ctx": along(row, -sense)}
    to_other, to_mate = {"ctx": other}, {"tp": mate}

    barrier = pltpu.get_barrier_semaphore()

    def greet(j, carry):
        pl.semaphore_signal(barrier, inc=1, device_id={"tp": me ^ j}, device_id_type=MESH)
        return carry

    lax.fori_loop(1, TP, greet, 0)
    for target in (to_ahead, to_behind, to_other):
        pl.semaphore_signal(barrier, inc=1, device_id=target, device_id_type=MESH)

    for p in range(PIECES):
        x_loads[p].wait()
        values = xbuf[p, me].astype(F32)
        stats[me, 0:1, p * PROWS : (p + 1) * PROWS] = to_lanes(
            jnp.sum(values * values, axis=1, keepdims=True)
        )
    stats[me, 1:2, :] = gain_ref[...].astype(F32).reshape(1, WIDTH)
    pl.semaphore_wait(barrier, TP - 1 + 3)

    push_start(stats, psend0, precv0)
    for p in range(PIECES):
        rows.start_sideways(p)
        rows.start_near(p)
    load_o.start()
    load_t.start()
    load_k.wait()
    load_v.wait()

    def share(base, whose, n):
        return pltpu.make_async_remote_copy(
            src_ref=wkv.at[half(base, whose)],
            dst_ref=wkv.at[half(base, whose)],
            send_sem=wsend.at[n],
            recv_sem=wrecv.at[n],
            device_id=to_mate,
            device_id_type=MESH,
        )

    share(0, core, 0).start()
    share(128, core, 1).start()
    push_wait(stats, psend0, precv0)
    squares = stats[0, 0:1, :]
    for slot in range(1, TP):
        squares = squares + stats[slot, 0:1, :]
    scale = lax.rsqrt(squares / D + EPS_IN)
    for p in range(PIECES):
        inv[p] = to_rows(scale[:, p * PROWS : (p + 1) * PROWS])
    accq[...] = jnp.zeros_like(accq)
    acckv[...] = jnp.zeros_like(acckv)

    load_q.wait()
    share(0, 1 - core, 0).wait_recv()
    share(128, 1 - core, 1).wait_recv()

    def consume(part, chip):
        at = pl.ds(pl.multiple_of(chip * 2 * WIDTH, 2 * WIDTH), 2 * WIDTH)
        both = []
        for slot in (2 * chip, 2 * chip + 1):
            gain = stats[slot, 1:2, :]
            for g in range(WIDTH // 128):
                lanes = slice(g * 128, (g + 1) * 128)
                column = []
                for p in (2 * part, 2 * part + 1):
                    values = xbuf[p, slot, :, lanes].astype(F32) * inv[p] * gain[:, lanes]
                    limit = CLIP_RATIO * jnp.max(jnp.abs(values), axis=-1, keepdims=True)
                    column.append(jnp.clip(values, -limit, limit).astype(BF16))
                both.append(jnp.concatenate(column, axis=0))
        quantized = jnp.concatenate(both, axis=1)
        accq[part] += jnp.dot(quantized, wq[at, :], preferred_element_type=F32)

        @pl.when(core == part)
        def _():
            acckv[...] += lax.dot_general(
                quantized, wkv[:, at], (((1,), (1,)), ((), ())), preferred_element_type=F32
            )

    def consume_all(part, kinds):
        chips = []
        for kind in kinds:
            for p in (2 * part, 2 * part + 1):
                rows.landed(p, 7 if kind is None else 8 + kind)
            chips.append((me if kind is None else rows.slots[kind]) // 2)

        def one(i, carry):
            consume(part, pick(chips, i))
            return carry

        lax.fori_loop(0, len(chips), one, 0)

    def kcopy(kind, block, part, target, g):
        return pltpu.make_async_remote_copy(
            src_ref=kvbuf.at[block, part, g],
            dst_ref=kvbuf.at[block, part, g],
            send_sem=ksend.at[g, kind],
            recv_sem=krecv.at[g, kind],
            device_id=target,
            device_id_type=MESH,
        )

    def klanded(kind, block, part, g):
        kcopy(kind, block, part, to_mate, g).wait_recv()

    def start_ring():
        for g in range(2):
            kcopy(0, ctx, core, to_ahead, g).start()
            kcopy(4, ctx, core, to_behind, g).start()
            kcopy(7, ctx, core, to_other, g).start()
            kcopy(15, ctx, core, to_mate, g).start()

    rings = {
        0: (0, -1, ((1, to_ahead), (8, to_other))),
        4: (0, 1, ((5, to_behind), (9, to_other))),
        1: (0, -2, ((2, to_ahead), (10, to_other))),
        5: (0, 2, ((6, to_behind), (11, to_other))),
        2: (0, -3, ((3, to_ahead),)),
        6: (0, 3, ()),
        3: (0, -4, ()),
        7: (1, 0, ()),
        8: (1, -1, ()),
        9: (1, 1, ()),
        10: (1, -2, ((12, to_ahead),)),
        11: (1, 2, ((14, to_behind),)),
        12: (1, -3, ((13, to_ahead),)),
        14: (1, 3, ()),
        13: (1, -4, ()),
    }

    def pass_on(*kinds):
        for g in range(2):
            for kind in kinds:
                far_row, delta, targets = rings[kind]
                block = along(1 - row if far_row else row, sense * delta)
                klanded(kind, block, core, g)
                for as_kind, target in targets:
                    kcopy(as_kind, block, core, target, g).start()
                kcopy(16 + kind, block, core, to_mate, g).start()

    rows.from_sides(0)
    rows.from_sides(1)
    rows.from_across(0)
    consume_all(0, (None,))
    rows.from_sides(2)
    rows.from_sides(3)
    rows.from_across(1)
    rows.from_across(2)
    rows.from_across(3)
    consume_all(1, (None,))
    consume_all(0, (0, 1))
    rows.from_far(0)
    rows.from_far(1)
    consume_all(0, (2,))
    rows.from_diagonal(0)
    consume_all(1, (0, 1))
    rows.from_far(2)
    rows.from_far(3)
    rows.from_far_across(0)
    consume_all(1, (2,))
    consume_all(0, (3,))
    rows.from_far_across(1)
    rows.from_diagonal(1)
    consume_all(1, (3,))
    consume_all(0, (4, 5, 6))

    def keep_kv():
        kvbuf[ctx, core] = acckv[...].astype(BF16).reshape(2, PROWS, 2 * HD)

    pl.when(core == 0)(keep_kv)
    rows.from_far_across(2)
    rows.from_diagonal(2)
    pl.when(core == 0)(start_ring)
    rows.from_far_across(3)
    consume_all(1, (6,))
    rows.from_diagonal(3)
    pl.when(core == 0)(functools.partial(pass_on, 0, 4))
    consume_all(1, (4, 5))
    pl.when(core == 1)(keep_kv)
    for part in range(2):
        for head in range(2):
            q[head * ROWS + part * HALF : head * ROWS + (part + 1) * HALF, :] = accq[
                part, :, head * HD : (head + 1) * HD
            ].astype(BF16)
    pl.when(core == 1)(start_ring)

    top[...] = jnp.full_like(top, FAR_BELOW)
    total[...] = jnp.zeros_like(total)
    acc[...] = jnp.zeros_like(acc)
    factor = HD ** (-0.5) * LOG2E

    def attend(keys, values, head, masked):
        at = slice(head * ROWS, (head + 1) * ROWS)
        scores = lax.dot_general(
            q[at, :], keys, (((1,), (1,)), ((), ())), preferred_element_type=F32
        )
        if masked:
            seen = lax.broadcasted_iota(jnp.int32, (ROWS, ROWS), 1) <= lax.broadcasted_iota(
                jnp.int32, (ROWS, ROWS), 0
            )
            scores = jnp.where(seen, scores, FAR_BELOW)
        high = jnp.max(scores, axis=-1, keepdims=True)
        before = top[at, :]
        now = jnp.maximum(before, jnp.broadcast_to(high, (ROWS, 128)))
        decay = jnp.exp2((before - now) * factor)
        shift = now * factor
        weights = []
        for g in range(ROWS // 128):
            lanes = slice(g * 128, (g + 1) * 128)
            part = jnp.exp2(scores[:, lanes] * factor - shift)
            if masked:
                part = jnp.where(seen[:, lanes], part, 0.0)
            weights.append(part)
        total[at, :] = decay * total[at, :] + ((weights[0] + weights[1]) + (weights[2] + weights[3]))
        mixed = jnp.dot(
            jnp.concatenate([part.astype(BF16) for part in weights], axis=1),
            values,
            preferred_element_type=F32,
        )
        acc[at, :] = decay * acc[at, :] + mixed
        top[at, :] = now

    def attend_block(block, masked):
        both = kvbuf[block].reshape(ROWS, 2 * HD)
        for head in range(2):
            attend(both[:, :HD], both[:, HD:], head, masked)

    order = (0, 4, 7, 1, 5, 8, 9, 2, 6, 10, 11, 3, 12, 14, 13)
    twin = {0: 4, 1: 5, 2: 6, 3: 3, 4: 0, 5: 1, 6: 2, 7: 7, 8: 9, 9: 8, 10: 11, 11: 10, 12: 14, 13: 13, 14: 12}

    def unit(j, carry):
        far_row = pick([jnp.int32(rings[kind][0]) for kind in order], j)
        delta = pick([jnp.int32(rings[kind][1]) for kind in order], j)
        kind = pick([jnp.int32(16 + twin[kind]) for kind in order], j)
        block = along(jnp.where(far_row == 1, 1 - row, row), sense * delta)
        for g in range(2):
            klanded(kind, block, 1 - core, g)

        @pl.when(block < ctx)
        def _():
            attend_block(block, False)

        return carry

    for g in range(2):
        klanded(15, ctx, 1 - core, g)
    attend_block(ctx, True)

    steps = ((0, 4), (7, 1, 5), (8, 9, 2, 6), (10, 11, 3), (12, 14), (13,))

    def ring_step(k, carry):
        for i, kinds in enumerate(steps):
            now = (k == i) & (core == 1) if i == 0 else k == i
            pl.when(now)(functools.partial(pass_on, *kinds))
        low = jnp.maximum(3 * k - 4, 0)
        high = jnp.minimum(jnp.maximum(3 * k - 1, 0), 15)
        lax.fori_loop(low, high, unit, 0)
        return carry

    lax.fori_loop(0, len(steps) + 1, ring_step, 0)

    heads = Gather(sbuf, ssend, srecv)
    for p in range(PIECES):
        for head in range(2):
            signs = (2 * sign_ref[head : head + 1, :] - 1).astype(F32)
            at = slice(head * ROWS + p * PROWS, head * ROWS + (p + 1) * PROWS)
            whole = jnp.sum(total[at, :], axis=-1, keepdims=True)
            attended = (acc[at, :] / whole).astype(BF16)
            sbuf[p, me, :, head * HD : (head + 1) * HD] = (
                attended.astype(F32) * signs
            ).astype(BF16)

    for p in range(PIECES):
        heads.start_sideways(p)
        heads.start_near(p)
    load_o.wait()
    load_t.wait()

    def rotate(p):
        heads.mates_landed(p, range(7, 15))

        def strip(i, carry):
            at = pl.ds(pl.multiple_of(i * STRIP, STRIP), STRIP)
            mix = []
            for slot in range(TP):
                both = sbuf[p, slot, at, :].astype(F32)
                mix += [both[:, :HD], both[:, HD:]]
            span = 1
            while span < QH:
                for h in range(QH):
                    if not h & span:
                        a, b = mix[h], mix[h + span]
                        mix[h], mix[h + span] = a + b, a - b
                span *= 2
            for h in range(QH):
                value = mix[h] * QH ** (-0.5)
                limit = CLIP_RATIO * jnp.max(jnp.abs(value), axis=-1, keepdims=True)
                rotated[p, at, h * HD : (h + 1) * HD] = jnp.clip(value, -limit, limit).astype(BF16)
            return carry

        lax.fori_loop(0, PROWS // STRIP, strip, 0)

    heads.from_sides(0)
    heads.from_sides(1)
    heads.from_across(0)
    heads.from_sides(2)
    heads.from_sides(3)
    heads.from_across(1)
    heads.from_across(2)
    heads.from_across(3)
    heads.from_far(0)
    heads.from_far(1)
    heads.from_diagonal(0)
    heads.from_far(2)
    heads.from_far(3)
    heads.from_diagonal(1)
    heads.from_far_across(0)
    rotate(0)
    heads.from_diagonal(2)
    heads.from_far_across(1)
    heads.from_diagonal(3)
    heads.from_far_across(2)
    rotate(1)
    heads.from_far_across(3)
    rotate(2)
    rotate(3)
    result = jnp.dot(
        rotated[...].reshape(ROWS, QH * HD), wo[...], preferred_element_type=F32
    )
    branch[...] = result.reshape(PIECES, PROWS, WIDTH)
    box1[me, 0:1, :] = to_lanes(jnp.sum(result * result, axis=1, keepdims=True))

    push_start(box1, psend1, precv1)
    rows.drain(PIECES)
    heads.drain(PIECES)
    share(0, core, 0).wait_send()
    share(128, core, 1).wait_send()

    def drain(kind, carry):
        for g in range(2):
            kcopy(kind, ctx, core, to_mate, g).wait_send()
        return carry

    lax.fori_loop(0, 31, drain, 0)
    push_wait(box1, psend1, precv1)
    squares = box1[0, 0:1, :]
    for slot in range(1, TP):
        squares = squares + box1[slot, 0:1, :]
    inverse = lax.rsqrt(squares / D + EPS_OUT)
    for p in range(PIECES):
        by_row = to_rows(inverse[:, p * PROWS : (p + 1) * PROWS])
        partial = jnp.zeros((PROWS, 128), F32)
        for g in range(WIDTH // 128):
            lanes = slice(g * 128, (g + 1) * 128)
            normal = branch[p, :, lanes] * by_row
            student[p, :, lanes] = normal.astype(BF16)
            difference = normal - teacher[p, :, lanes].astype(F32)
            partial = partial + difference * difference
        box2[me, 0:1, p * PROWS : (p + 1) * PROWS] = to_lanes(
            jnp.sum(partial, axis=1, keepdims=True)
        )
    push_start(box2, psend2, precv2)
    store = pltpu.make_async_copy(student, student_hbm, x_sem.at[0])
    store.start()
    push_wait(box2, psend2, precv2)
    loss = box2[0, 0:1, :]
    for slot in range(1, TP):
        loss = loss + box2[slot, 0:1, :]
    loss_ref[...] = loss / D
    store.wait()


def block(x, gain, w_query, w_key, w_value, sign_bits, w_out, teacher):
    any_space = pl.BlockSpec(memory_space=pl.ANY)
    vmem = pl.BlockSpec(memory_space=pltpu.VMEM)
    dma = pltpu.SemaphoreType.DMA
    return pl.pallas_call(
        block_kernel,
        out_shape=(
            jax.ShapeDtypeStruct((PIECES, PROWS, WIDTH), BF16),
            jax.ShapeDtypeStruct((1, ROWS), F32),
        ),
        in_specs=[any_space, vmem, any_space, any_space, any_space, vmem, any_space, any_space],
        out_specs=(any_space, vmem),
        scratch_shapes=[
            pltpu.VMEM((PIECES, TP, PROWS, WIDTH), BF16),
            pltpu.VMEM((TP, 2, ROWS), F32),
            pltpu.VMEM((D, 256), BF16),
            pltpu.VMEM((256, D), BF16),
            pltpu.VMEM((PIECES, PROWS, 128), F32),
            pltpu.VMEM((2, HALF, 256), F32),
            pltpu.VMEM((HALF, 256), F32),
            pltpu.VMEM((QROWS, HD), BF16),
            pltpu.VMEM((16, 2, 2, PROWS, 2 * HD), BF16),
            pltpu.VMEM((QROWS, 128), F32),
            pltpu.VMEM((QROWS, 128), F32),
            pltpu.VMEM((QROWS, HD), F32),
            pltpu.VMEM((PIECES, TP, PROWS, 2 * HD), BF16),
            pltpu.VMEM((QH * HD, WIDTH), BF16),
            pltpu.VMEM((PIECES, PROWS, QH * HD), BF16),
            pltpu.VMEM((PIECES, PROWS, WIDTH), F32),
            pltpu.VMEM((PIECES, PROWS, WIDTH), BF16),
            pltpu.VMEM((PIECES, PROWS, WIDTH), BF16),
            pltpu.VMEM((TP, 1, ROWS), F32),
            pltpu.VMEM((TP, 1, ROWS), F32),
            dma((PIECES, 15)),
            dma((PIECES, 15)),
            dma((2, 31)),
            dma((2, 31)),
            dma((PIECES, 15)),
            dma((PIECES, 15)),
            dma((TP,)),
            dma((TP,)),
            dma((TP,)),
            dma((TP,)),
            dma((TP,)),
            dma((TP,)),
            dma((2,)),
            dma((2,)),
            dma((5,)),
            dma((PIECES,)),
        ],
        compiler_params=pltpu.CompilerParams(
            collective_id=0, has_side_effects=True, vmem_limit_bytes=VMEM_LIMIT
        ),
        name="block",
    )(
        x.reshape(PIECES, PROWS, WIDTH),
        gain,
        w_query,
        w_key.T,
        w_value.T,
        sign_bits,
        w_out,
        teacher.reshape(PIECES, PROWS, WIDTH),
    )


def hand_over_kernel(student_ref, loss_ref, student_out, loss_out):
    student_out[...] = student_ref[...]
    loss_out[...] = loss_ref[...].reshape(ROWS)


def hand_over(student, loss):
    vmem = pl.BlockSpec(memory_space=pltpu.VMEM)
    return pl.pallas_call(
        hand_over_kernel,
        out_shape=(
            jax.ShapeDtypeStruct((ROWS, WIDTH), BF16),
            jax.ShapeDtypeStruct((ROWS,), F32),
        ),
        in_specs=[vmem, vmem],
        out_specs=(vmem, vmem),
        name="hand_over",
    )(student.reshape(ROWS, WIDTH), loss)


def body(*arguments):
    return hand_over(*block(*arguments))


def solution(mesh):
    in_specs = (
        P("ctx", "tp"),
        P("tp"),
        P(None, "tp"),
        P(None, "tp"),
        P(None, "tp"),
        P("tp", None),
        P(None, "tp"),
        P("ctx", "tp"),
    )
    out_specs = (P("ctx", "tp"), P("ctx"))
    return jax.shard_map(body, mesh=mesh, in_specs=in_specs, out_specs=out_specs, check_vma=False)
```
